32 devices in a mesh: expert: 8 (over y, x, core), dp: 4 (over z).
Axes of the slice: x: 2, y: 2, z: 4, core: 2. Of those that a mesh axis runs over, the one named last changes fastest.
Arguments:
- tokens: bfloat16 [6144, 1024], P(('expert', 'dp')), may hold values from -6 to 6
- grad_out: bfloat16 [6144, 1024], P(('expert', 'dp')), may hold values from -6 to 6
- routes: int32 [6144, 2], P(('expert', 'dp')), may hold values from 0 to 7, all different within a row
- keep_second: int32 [6144], P(('expert', 'dp')), may hold values 0 or 1
- combine: bfloat16 [6144, 2], P(('expert', 'dp')), may hold values from 0.099609375 to 0.8984375
- w_in: bfloat16 [8, 2048, 1024], P('expert'), may hold values from -0.1875 to 0.1875
- w_out: bfloat16 [8, 2048, 1024], P('expert'), may hold values from -0.125 to 0.125
Outputs:
- grad_tokens: bfloat16 [6144, 1024], P(('expert', 'dp'))
- grad_combine: bfloat16 [6144, 2], P(('expert', 'dp'))
- grad_w_in: float32 [8, 2048, 1024], P('expert', 'dp')
- grad_w_out: float32 [8, 2048, 1024], P('expert', 'dp')
The draws below stay inside these ranges and needn't reach their ends.
Inputs may be any that keep to these rules, and one draw needn't show every extreme that they name: `routes`: each token names two different experts.
All inputs are finite; a program needn't handle non-finite values. No bound on the sum of `keep_second` on one device may be relied on, other than what follows from the above.
Results may differ from the reference program's by a relative error of at most 0.011.
Values may be sent and summed in bfloat16 or wider, within the bound.
No kernel may reach another device: no remote copies, remote signals or barrier semaphores. Data moves between devices by JAX's collectives and lax.ppermute only.
A program may use at most 128 MiB of HBM per device.

```python
import jax
import jax.numpy as jnp
from jax import lax

D = 1024
FF = 2048
TOK_DEV = 192
EXPERTS = 8
TOKENS = 6144
CAP = 60
N_EXPERT = 8
N_DP = 4


def place_ends(drawn, own_key, smallest, largest):
    extent = drawn.shape
    spot = [jax.random.randint(jax.random.fold_in(own_key, axis), (), 0, extent[axis]) for axis in range(len(extent))]
    drawn = drawn.at[tuple(spot)].set(smallest)
    longest = extent.index(max(extent))
    spot[longest] = (spot[longest] + 1) % extent[longest]
    return drawn.at[tuple(spot)].set(largest)


def block_scale(rng, extent, cuts, smallest, top_value):
    def one(dim, parts):
        draws = jax.random.uniform(jax.random.fold_in(jax.random.fold_in(rng, 6), dim), (parts,), jnp.float32, smallest / len(cuts), top_value / len(cuts))
        return jnp.repeat(jnp.exp(draws), extent[dim] // parts).reshape((-1,) + (1,) * (len(extent) - dim - 1))

    gain = one(*cuts[0])
    for cut in cuts[1:]:
        gain = gain * one(*cut)
    return gain


def distinct(key, rows, number_of, top, lift):
    sequence = jax.random.permutation(jax.random.fold_in(key, 1), number_of)
    pull = sequence
    for power in range(3):
        pull = pull * pull // number_of
    pull = pull * lift // number_of
    tickets = jax.random.randint(jax.random.fold_in(key, 2), (rows, number_of), 0, 4096) + pull
    holders = jax.random.permutation(jax.random.fold_in(key, 3), rows)[jnp.arange(number_of) % rows]
    tickets = jnp.where(jnp.arange(rows)[:, None] == holders[None, :], 1 << 14, tickets)
    score = tickets * number_of + jnp.arange(number_of)
    return lax.top_k(score.astype(jnp.int32), top)[1].astype(jnp.int32)


def normal_values(own_key, extent, deviation, most, shards=(), kind=jnp.bfloat16):
    gain = block_scale(own_key, extent, shards, -0.22, 0.18) if shards else 1.0
    entries = jax.random.normal(own_key, extent, jnp.float32) * deviation * gain
    return jnp.minimum(jnp.maximum(entries, -most), most).astype(kind)


def setup_inputs(seed: int = 0) -> dict:
    streams_of = jax.random.split(jax.random.key(seed), 8)
    return {
        "tokens": normal_values(streams_of[0], (TOKENS, D), 1.0, 6.0, ((0, 32),)),
        "grad_out": normal_values(streams_of[1], (TOKENS, D), 1.0, 6.0, ((0, 32),)),
        "routes": distinct(streams_of[2], TOKENS, EXPERTS, 2, 4096),
        "keep_second": place_ends((jax.random.randint(streams_of[3], (TOKENS,), 0, 4) < 3).astype(jnp.int32), jax.random.fold_in(streams_of[3], 1), 0, 1),
        "combine": jnp.clip(0.099609375 + 0.7988281 * jax.random.uniform(streams_of[4], (TOKENS, 2), jnp.float32) ** block_scale(streams_of[4], (TOKENS, 2), ((0, 32),), -0.2, 0.2), 0.099609375, 0.8984375).astype(jnp.bfloat16),
        "w_in": normal_values(streams_of[5], (EXPERTS, FF, D), D ** -0.5, 0.1875, ((0, 8),)),
        "w_out": normal_values(streams_of[6], (EXPERTS, FF, D), FF ** -0.5, 0.125, ((0, 8),)),
    }


root_coef = 0.7978845608
cube_coef = 0.044715


def gelu_slope(hidden):
    inner_arg = root_coef * (hidden + cube_coef * hidden * hidden * hidden)
    tanh_val = jnp.tanh(inner_arg)
    active = 0.5 * hidden * (1.0 + tanh_val)
    derivative = 0.5 * (1.0 + tanh_val) + 0.5 * hidden * (1.0 - tanh_val * tanh_val) * root_coef * (1.0 + 3.0 * cube_coef * hidden * hidden)
    return active, derivative


def slot_index(routes, keep_second, expert_count, capacity):
    expert_ids = jnp.arange(expert_count, dtype=jnp.int32)
    first_hot = (routes[:, 0:1] == expert_ids[None, :]).astype(jnp.int32)
    second_hot = (routes[:, 1:2] == expert_ids[None, :]).astype(jnp.int32) * keep_second[:, None]
    first_pos = jnp.cumsum(first_hot, axis=0).astype(jnp.int32) - first_hot
    second_pos = jnp.cumsum(second_hot, axis=0).astype(jnp.int32) - second_hot + jnp.sum(first_hot, axis=0).astype(jnp.int32)[None, :]
    first_slot = jnp.sum(first_pos * first_hot, axis=1).astype(jnp.int32)
    second_slot = jnp.sum(second_pos * second_hot, axis=1).astype(jnp.int32)
    first_flat = jnp.where(first_slot < capacity, routes[:, 0] * capacity + first_slot, -1).astype(jnp.int32)
    second_live = (keep_second > 0) & (second_slot < capacity)
    second_flat = jnp.where(second_live, routes[:, 1] * capacity + second_slot, -1).astype(jnp.int32)
    slot_ids = jnp.arange(expert_count * capacity, dtype=jnp.int32)
    first_pick = slot_ids[:, None] == first_flat[None, :]
    second_pick = slot_ids[:, None] == second_flat[None, :]
    return first_pick, second_pick


def dispatch(tokens, grad_out, combine, first_pick, second_pick):
    chosen = (first_pick | second_pick).astype(jnp.bfloat16)
    sent_x = jnp.dot(chosen, tokens, preferred_element_type=jnp.float32).astype(jnp.bfloat16)
    sent_dy = jnp.dot(chosen, grad_out, preferred_element_type=jnp.float32).astype(jnp.bfloat16)
    weights = combine.astype(jnp.float32)
    sent_c = jnp.sum(jnp.where(first_pick, weights[None, :, 0], 0.0) + jnp.where(second_pick, weights[None, :, 1], 0.0), axis=1).astype(jnp.bfloat16)
    return sent_x, sent_dy, sent_c


def expert_rows(rows_x, rows_dy, rows_c, weight_in, weight_out):
    hidden = lax.dot_general(rows_x, weight_in, (((1,), (1,)), ((), ())), preferred_element_type=jnp.float32)
    active, derivative = gelu_slope(hidden)
    active_b = active.astype(jnp.bfloat16)
    output = jnp.dot(active_b, weight_out, preferred_element_type=jnp.float32)
    gate_grad = jnp.sum(output * rows_dy.astype(jnp.float32), axis=1).astype(jnp.bfloat16)
    scaled = (rows_c.astype(jnp.float32)[:, None] * rows_dy.astype(jnp.float32)).astype(jnp.bfloat16)
    active_grad = lax.dot_general(scaled, weight_out, (((1,), (1,)), ((), ())), preferred_element_type=jnp.float32)
    hidden_grad = (active_grad * derivative).astype(jnp.bfloat16)
    token_grad = jnp.dot(hidden_grad, weight_in, preferred_element_type=jnp.float32).astype(jnp.bfloat16)
    return token_grad, gate_grad, hidden_grad, active_b, scaled


def collect(token_back, gate_back, first_pick, second_pick):
    chosen = (first_pick | second_pick).astype(jnp.bfloat16)
    grad_tokens = lax.dot_general(chosen, token_back, (((0,), (0,)), ((), ())), preferred_element_type=jnp.float32).astype(jnp.bfloat16)
    gate_float = gate_back.astype(jnp.float32)[:, None]
    first_grad = jnp.sum(jnp.where(first_pick, gate_float, 0.0), axis=0)
    second_grad = jnp.sum(jnp.where(second_pick, gate_float, 0.0), axis=0)
    grad_combine = jnp.stack([first_grad, second_grad], axis=1).astype(jnp.bfloat16)
    return grad_tokens, grad_combine


def expert_full(bundle):
    rows_x, rows_dy, rows_c, weight_in, weight_out = bundle
    token_grad, gate_grad, hidden_grad, active_b, scaled = expert_rows(rows_x, rows_dy, rows_c, weight_in, weight_out)
    grad_in = lax.dot_general(hidden_grad, rows_x, (((0,), (0,)), ((), ())), preferred_element_type=jnp.float32)
    grad_outw = lax.dot_general(active_b, scaled, (((0,), (0,)), ((), ())), preferred_element_type=jnp.float32)
    return token_grad, gate_grad, grad_in, grad_outw


def regroup(array):
    shaped = array.reshape((N_EXPERT, N_DP, TOK_DEV) + array.shape[1:])
    return jnp.swapaxes(shaped, 0, 1)


def reference(tokens, grad_out, routes, keep_second, combine, w_in, w_out):
    capacity = CAP

    def one_group(totals, group_data):
        group_x, group_dy, group_routes, group_keep, group_combine = group_data
        first_pick, second_pick = jax.vmap(slot_index, in_axes=(0, 0, None, None))(group_routes, group_keep, EXPERTS, capacity)
        sent_x, sent_dy, sent_c = jax.vmap(dispatch)(group_x, group_dy, group_combine, first_pick, second_pick)
        rows_x = jnp.swapaxes(sent_x.reshape(N_EXPERT, EXPERTS, capacity, D), 0, 1).reshape(EXPERTS, N_EXPERT * capacity, D)
        rows_dy = jnp.swapaxes(sent_dy.reshape(N_EXPERT, EXPERTS, capacity, D), 0, 1).reshape(EXPERTS, N_EXPERT * capacity, D)
        rows_c = jnp.swapaxes(sent_c.reshape(N_EXPERT, EXPERTS, capacity), 0, 1).reshape(EXPERTS, N_EXPERT * capacity)
        token_grad, gate_grad, grad_in, grad_outw = lax.map(expert_full, (rows_x, rows_dy, rows_c, w_in, w_out))
        token_back = jnp.swapaxes(token_grad.reshape(EXPERTS, N_EXPERT, capacity, D), 0, 1).reshape(N_EXPERT, EXPERTS * capacity, D)
        gate_back = jnp.swapaxes(gate_grad.reshape(EXPERTS, N_EXPERT, capacity), 0, 1).reshape(N_EXPERT, EXPERTS * capacity)
        grad_part, combine_part = jax.vmap(collect)(token_back, gate_back, first_pick, second_pick)
        return (totals[0] + grad_in, totals[1] + grad_outw), (grad_part, combine_part)

    zero_grad = jnp.zeros((EXPERTS, FF, D), jnp.float32)
    streams = (regroup(tokens), regroup(grad_out), regroup(routes), regroup(keep_second), regroup(combine))
    sums, pieces = lax.scan(one_group, (zero_grad, zero_grad), streams)
    grad_tokens = jnp.swapaxes(pieces[0], 0, 1).reshape(N_EXPERT * N_DP * TOK_DEV, D)
    grad_combine = jnp.swapaxes(pieces[1], 0, 1).reshape(N_EXPERT * N_DP * TOK_DEV, 2)
    return grad_tokens, grad_combine, sums[0], sums[1]
```

```python
import functools

import jax
import jax.numpy as jnp
from jax import lax
from jax.experimental import pallas as pl
from jax.experimental.pallas import tpu as pltpu
from jax.sharding import PartitionSpec as P


root_coef = 0.7978845608
cube_coef = 0.044715
bf16 = jnp.bfloat16
f32 = jnp.float32

NN = (((1,), (0,)), ((), ()))
NT = (((1,), (1,)), ((), ()))
TN = (((0,), (0,)), ((), ()))


def dot(a, b, dims=NN):
    return lax.dot_general(a, b, dims, preferred_element_type=f32)


def gelu_slope(hidden):
    square = hidden * hidden
    tanh_val = jnp.tanh(root_coef * (hidden + cube_coef * square * hidden))
    half_up = 0.5 * (1.0 + tanh_val)
    active = hidden * half_up
    derivative = half_up + 0.5 * hidden * (1.0 - tanh_val * tanh_val) * root_coef * (
        1.0 + 3.0 * cube_coef * square
    )
    return active, derivative


def steps(extent, most):
    size = min(extent, most)
    return [(at, size) for at in range(0, extent, size)]


def stack(refs, part, block):
    return jnp.concatenate([ref[part * block : (part + 1) * block, :] for ref in refs], axis=0)


def slot_rows(routes, keep, combine, me, experts, block, capacity):
    count = routes.shape[1]
    kept = keep > 0
    first, second = routes[0:1, :] ^ me, routes[1:2, :] ^ me
    ids = lax.broadcasted_iota(jnp.int32, (experts, count), 0)
    first_hot = jnp.where(first == ids, 1.0, 0.0)
    second_hot = jnp.where((second == ids) & kept, 1.0, 0.0)
    earlier = jnp.where(
        lax.broadcasted_iota(jnp.int32, (count, count), 0)
        < lax.broadcasted_iota(jnp.int32, (count, count), 1),
        1.0,
        0.0,
    ).astype(bf16)
    first_pos = dot(first_hot.astype(bf16), earlier)
    second_pos = dot(second_hot.astype(bf16), earlier) + jnp.sum(first_hot, axis=1, keepdims=True)
    first_slot = jnp.sum(first_pos * first_hot, axis=0, keepdims=True)
    second_slot = jnp.sum(second_pos * second_hot, axis=0, keepdims=True)
    first_flat = jnp.where(first_slot < capacity, first.astype(f32) * block + first_slot, -1.0)
    second_flat = jnp.where(
        kept & (second_slot < capacity), second.astype(f32) * block + second_slot, -1.0
    )
    weights = combine.astype(f32)
    return first_flat, second_flat, weights[0:1, :], weights[1:2, :]


def picks(first_flat, second_flat, rows):
    ids = lax.broadcasted_iota(jnp.int32, (rows, first_flat.shape[1]), 0)
    return ids == first_flat.astype(jnp.int32), ids == second_flat.astype(jnp.int32)


def place(pick, source_ref, out_refs, part, block):
    for at, size in steps(source_ref.shape[1], 256):
        rows = dot(pick, source_ref[:, at : at + size]).astype(bf16)
        for k, out in enumerate(out_refs):
            out[part * block : (part + 1) * block, at : at + size] = rows[
                k * block : (k + 1) * block
            ]


def own_send_kernel(
    experts, block, capacity, pos, routes, keep, combine, tokens, grad_out, meta, *outs
):
    a, b, c, d = slot_rows(
        routes[...], keep[...], combine[...], pos[0], experts, block, capacity
    )
    meta[0:1, :] = a
    meta[1:2, :] = b
    meta[2:3, :] = c
    meta[3:4, :] = d
    meta[4:8, :] = jnp.zeros((4, a.shape[1]), f32)
    first, second = picks(a, b, experts * block)
    chosen = jnp.where(first | second, 1.0, 0.0).astype(bf16)
    place(chosen, tokens, outs, 0, block)
    weighted = jnp.where(first, c, jnp.where(second, d, 0.0)).astype(bf16)
    place(weighted, grad_out, outs, 1, block)


def send_x_kernel(experts, block, meta, tokens, *outs):
    first, second = picks(meta[0:1, :], meta[1:2, :], experts * block)
    place(jnp.where(first | second, 1.0, 0.0).astype(bf16), tokens, outs, 0, block)


def send_s_kernel(experts, block, meta, grad_out, *outs):
    first, second = picks(meta[0:1, :], meta[1:2, :], experts * block)
    weighted = jnp.where(first, meta[2:3, :], jnp.where(second, meta[3:4, :], 0.0)).astype(bf16)
    place(weighted, grad_out, outs, 0, block)


def put_tokens(hidden_grad, w_in, gates, outs, block, capacity):
    gate_rows = gates.astype(bf16)
    for at, size in steps(w_in.shape[-1], 256):
        rows = dot(hidden_grad, w_in[0, :, at : at + size], TN).astype(bf16)
        for k, out in enumerate(outs):
            out[:, at : at + size] = rows[k * block : (k + 1) * block]
    for k, out in enumerate(outs):
        out[capacity : capacity + 1, 0:block] = gate_rows[:, k * block : (k + 1) * block]


def own_expert_kernel(experts, block, capacity, pos, w_in, w_out, *refs):
    blocks, (act, grad), outs = refs[:experts], refs[experts : experts + 2], refs[experts + 2 :]
    x, s = stack(blocks, 0, block), stack(blocks, 1, block)
    gates = 0.0
    for at, size in steps(w_in.shape[1], 256):
        active, slope = gelu_slope(dot(w_in[0, at : at + size, :], x, NT))
        active = active.astype(bf16)
        act[at : at + size, :] = active
        up = dot(w_out[0, at : at + size, :], s, NT)
        gates = gates + jnp.sum(active.astype(f32) * up, axis=0, keepdims=True)
        grad[at : at + size, :] = (up * slope).astype(bf16)
    put_tokens(grad[...], w_in, gates, outs, block, capacity)


def act_kernel(experts, block, pos, w_in, *refs):
    blocks, (act, slope) = refs[:experts], refs[experts:]
    x = stack(blocks, 0, block)
    for at, size in steps(w_in.shape[1], 256):
        active, derivative = gelu_slope(dot(w_in[0, at : at + size, :], x, NT))
        act[at : at + size, :] = active.astype(bf16)
        slope[at : at + size, :] = derivative.astype(bf16)


def grad_kernel(experts, block, pos, w_out, act, slope, *refs):
    blocks, (grad, gates) = refs[:experts], refs[experts:]
    s = stack(blocks, 0, block)
    total = 0.0
    for at, size in steps(w_out.shape[1], 256):
        up = dot(w_out[0, at : at + size, :], s, NT)
        total = total + jnp.sum(act[at : at + size, :].astype(f32) * up, axis=0, keepdims=True)
        grad[at : at + size, :] = (up * slope[at : at + size, :].astype(f32)).astype(bf16)
    gates[...] = jnp.broadcast_to(total, gates.shape)


def tokens_kernel(experts, block, capacity, pos, w_in, grad, gates, *outs):
    put_tokens(grad[...], w_in, gates[0:1, :], outs, block, capacity)


def outer_rows(own_ref, other_ref, own_rows, other_rows, at, size):
    return dot(own_ref[pl.ds(at, size), :], own_rows) + dot(other_ref[pl.ds(at, size), :], other_rows)


def away_kernel(experts, block, part, owners, pos, own, other, *refs):
    own_blocks, other_blocks, outs = refs[:experts], refs[experts : 2 * experts], refs[2 * experts :]
    own_rows, other_rows = stack(own_blocks, part, block), stack(other_blocks, 0, block)
    size = own.shape[0] // owners
    for r, out in enumerate(outs):
        at = pl.multiple_of(lax.rem(pos[2] + r + 1, owners) * size, size)
        out[...] = outer_rows(own, other, own_rows, other_rows, at, size).astype(bf16)


def home_kernel(experts, block, part, owners, pos, own, other, *refs):
    own_blocks, other_blocks = refs[:experts], refs[experts : 2 * experts]
    got, out = refs[2 * experts : -1], refs[-1]
    own_rows, other_rows = stack(own_blocks, part, block), stack(other_blocks, 0, block)
    size = own.shape[0] // owners
    at = pl.multiple_of(pos[2] * size, size)
    total = outer_rows(own, other, own_rows, other_rows, at, size)
    for ref in got:
        total = total + ref[...].astype(f32)
    out[0] = total


def gathered(meta, refs, experts, block, capacity):
    first, second = picks(meta[0:1, :], meta[1:2, :], experts * block)
    chosen = jnp.where(first | second, 1.0, 0.0).astype(bf16)
    rows = stack(refs, 0, block)
    tokens = dot(chosen, rows, TN)
    gates = [ref[capacity : capacity + 1, 0:block] for ref in refs]
    values = jnp.concatenate(gates, axis=0)
    out = []
    for at in (0, 1):
        flat = meta[at : at + 1, :].astype(jnp.int32)
        live = flat >= 0
        which = jnp.where(live, flat, 0) // block
        where = flat - which * block
        lane = lax.broadcasted_iota(jnp.int32, (block, flat.shape[1]), 0)
        hit = jnp.where((lane == where) & live, 1.0, 0.0).astype(bf16)
        by_block = dot(values, hit)
        mine = lax.broadcasted_iota(jnp.int32, by_block.shape, 0) == which
        gate = jnp.sum(jnp.where(mine, by_block, 0.0), axis=0, keepdims=True)
        out.append(jnp.where(live, gate / meta[at + 2 : at + 3, :], 0.0))
    return tokens, out


def other_collect_kernel(experts, block, capacity, meta, *refs):
    blocks, out = refs[:experts], refs[experts]
    tokens, gates = gathered(meta, blocks, experts, block, capacity)
    count = tokens.shape[0]
    out[0:count, :] = tokens.astype(bf16)
    pad = jnp.concatenate(
        [g for g in gates] + [jnp.zeros((14, count), f32)], axis=0
    )
    out[count : count + 16, 0:count] = pad.astype(bf16)


def own_collect_kernel(experts, block, capacity, meta, got, *refs):
    blocks, (grad_tokens, grad_combine) = refs[:experts], refs[experts:]
    tokens, gates = gathered(meta, blocks, experts, block, capacity)
    count = tokens.shape[0]
    grad_tokens[...] = (tokens + got[0:count, :].astype(f32)).astype(bf16)
    more = got[count : count + 16, 0:count].astype(f32)
    grad_combine[...] = (jnp.concatenate(gates, axis=0) + more[0:2, :]).astype(bf16)


def shaped(shape, dtype=bf16):
    return jax.ShapeDtypeStruct(shape, dtype)


def whole(count):
    return [pl.BlockSpec(memory_space=pltpu.VMEM)] * count


def call(kernel, name, outs, scalars, arrays, flops=0, halves=()):
    halves = list(halves)
    specs = []
    for i, array in enumerate(arrays):
        if i in halves:
            extent = (1, array.shape[1] // 2, array.shape[2])
            specs.append(pl.BlockSpec(extent, lambda g, pos: (0, pos[1], 0)))
        else:
            specs.append(
                pl.BlockSpec(array.shape, lambda g, *pos, rank=array.ndim: (0,) * rank)
            )
    out_specs = [
        pl.BlockSpec(out.shape, lambda g, *pos, rank=len(out.shape): (0,) * rank) for out in outs
    ]
    moved = sum(a.size * a.dtype.itemsize for a in arrays)
    grid_spec = pltpu.PrefetchScalarGridSpec(
        num_scalar_prefetch=len(scalars), grid=(1,), in_specs=specs, out_specs=out_specs
    )
    return pl.pallas_call(
        kernel,
        name=name,
        out_shape=outs,
        grid_spec=grid_spec,
        cost_estimate=pl.CostEstimate(flops=int(flops), transcendentals=0, bytes_accessed=moved),
    )(*scalars, *arrays)


def per_device(tokens, grad_out, routes, keep_second, combine, w_in, w_out):
    experts, planes = lax.axis_size("expert"), lax.axis_size("dp")
    count, width = tokens.shape
    capacity = 5 * count // (2 * experts)
    block = -(-(capacity + 1) // 16) * 16
    owners = planes // 2
    units = w_in.shape[1] // 2
    rows = experts * block
    if planes % 2 or experts & (experts - 1):
        raise ValueError("mesh sizes")
    me, plane = lax.axis_index("expert"), lax.axis_index("dp")
    pos = jnp.stack([me, plane // owners, plane % owners]).astype(jnp.int32)
    bind = functools.partial

    def across(value):
        return lax.ppermute(value, "dp", [(j, (j + owners) % planes) for j in range(planes)])

    def exchange(values):
        return [values[0]] + [
            lax.ppermute(values[k], "expert", [(i, i ^ k) for i in range(experts)])
            for k in range(1, experts)
        ]

    def to_owners(values):
        return [
            lax.ppermute(
                value,
                "dp",
                [(j, j // owners * owners + (j + r + 1) % owners) for j in range(planes)],
            )
            for r, value in enumerate(values)
        ]

    with jax.named_scope("z_x"):
        other_x = across(tokens)
    with jax.named_scope("z_dy"):
        other_dy = across(grad_out)
    with jax.named_scope("own_send"):
        meta, *own_blocks = call(
            bind(own_send_kernel, experts, block, capacity),
            "own_send",
            [shaped((8, count), f32)] + [shaped((2 * block, width))] * experts,
            [pos],
            [routes.T, keep_second.reshape(1, count), combine.T, tokens, grad_out],
            4 * rows * count * width,
        )
    with jax.named_scope("z_meta"):
        other_meta = across(meta)
    with jax.named_scope("own_out"):
        own_blocks = exchange(own_blocks)
    with jax.named_scope("send_x"):
        other_xb = call(
            bind(send_x_kernel, experts, block),
            "send_x",
            [shaped((block, width))] * experts,
            [],
            [other_meta, other_x],
            2 * rows * count * width,
        )
    with jax.named_scope("x_out"):
        other_xb = exchange(other_xb)
    with jax.named_scope("send_s"):
        other_sb = call(
            bind(send_s_kernel, experts, block),
            "send_s",
            [shaped((block, width))] * experts,
            [],
            [other_meta, other_dy],
            2 * rows * count * width,
        )
    with jax.named_scope("s_out"):
        other_sb = exchange(other_sb)
    with jax.named_scope("own_expert"):
        own_act, own_grad, *own_back = call(
            bind(own_expert_kernel, experts, block, capacity),
            "own_expert",
            [shaped((units, rows))] * 2 + [shaped((block, width))] * experts,
            [pos],
            [w_in, w_out] + own_blocks,
            6 * rows * units * width,
            (0, 1),
        )
    with jax.named_scope("other_act"):
        other_act, other_slope = call(
            bind(act_kernel, experts, block),
            "other_act",
            [shaped((units, rows))] * 2,
            [pos],
            [w_in] + other_xb,
            2 * rows * units * width,
            (0,),
        )
    share = units // owners
    with jax.named_scope("away_out"):
        away_out = call(
            bind(away_kernel, experts, block, 1, owners),
            "away_out",
            [shaped((share, width))] * (owners - 1),
            [pos],
            [own_act, other_act] + own_blocks + other_sb,
            4 * rows * share * (owners - 1) * width,
        )
    with jax.named_scope("rs_out"):
        got_out = to_owners(away_out)
    with jax.named_scope("other_grad"):
        other_grad, gates = call(
            bind(grad_kernel, experts, block),
            "other_grad",
            [shaped((units, rows)), shaped((8, rows), f32)],
            [pos],
            [w_out, other_act, other_slope] + other_sb,
            2 * rows * units * width,
            (0,),
        )
    with jax.named_scope("away_in"):
        away_in = call(
            bind(away_kernel, experts, block, 0, owners),
            "away_in",
            [shaped((share, width))] * (owners - 1),
            [pos],
            [own_grad, other_grad] + own_blocks + other_xb,
            4 * rows * share * (owners - 1) * width,
        )
    with jax.named_scope("rs_in"):
        got_in = to_owners(away_in)
    with jax.named_scope("other_tokens"):
        other_back = call(
            bind(tokens_kernel, experts, block, capacity),
            "other_tokens",
            [shaped((block, width))] * experts,
            [pos],
            [w_in, other_grad, gates],
            2 * rows * units * width,
            (0,),
        )
    with jax.named_scope("other_ret"):
        other_back = exchange(other_back)
    with jax.named_scope("own_ret"):
        own_back = exchange(own_back)
    with jax.named_scope("other_collect"):
        other_part = call(
            bind(other_collect_kernel, experts, block, capacity),
            "other_collect",
            [shaped((count + 16, width))],
            [],
            [other_meta] + other_back,
            2 * rows * count * width,
        )[0]
    with jax.named_scope("z_ret"):
        part = across(other_part)
    with jax.named_scope("home_out"):
        grad_outw = call(
            bind(home_kernel, experts, block, 1, owners),
            "home_out",
            [shaped((1, share, width), f32)],
            [pos],
            [own_act, other_act] + own_blocks + other_sb + got_out,
            4 * rows * share * width,
        )[0]
    with jax.named_scope("own_collect"):
        grad_tokens, grad_combine = call(
            bind(own_collect_kernel, experts, block, capacity),
            "own_collect",
            [shaped((count, width)), shaped((2, count))],
            [],
            [meta, part] + own_back,
            2 * rows * count * width,
        )
    with jax.named_scope("home_in"):
        grad_in = call(
            bind(home_kernel, experts, block, 0, owners),
            "home_in",
            [shaped((1, share, width), f32)],
            [pos],
            [own_grad, other_grad] + own_blocks + other_xb + got_in,
            4 * rows * share * width,
        )[0]
    return grad_tokens, grad_combine.T, grad_in, grad_outw


def solution(mesh):
    return jax.shard_map(
        per_device,
        mesh=mesh,
        in_specs=(
            P(("expert", "dp"), None),
            P(("expert", "dp"), None),
            P(("expert", "dp"), None),
            P(("expert", "dp")),
            P(("expert", "dp"), None),
            P("expert", None, None),
            P("expert", None, None),
        ),
        out_specs=(
            P(("expert", "dp"), None),
            P(("expert", "dp"), None),
            P("expert", "dp", None),
            P("expert", "dp", None),
        ),
        check_vma=False,
    )
```

```python
import functools

import jax
import jax.numpy as jnp
from jax import lax
from jax.experimental import pallas as pl
from jax.experimental.pallas import tpu as pltpu
from jax.sharding import PartitionSpec as P


root_coef = 0.7978845608
cube_coef = 0.044715
bf16 = jnp.bfloat16
f32 = jnp.float32

NN = (((1,), (0,)), ((), ()))
NT = (((1,), (1,)), ((), ()))
TN = (((0,), (0,)), ((), ()))


def dot(a, b, dims=NN):
    return lax.dot_general(a, b, dims, preferred_element_type=f32)


def gelu_slope(hidden):
    square = hidden * hidden
    tanh_val = jnp.tanh(hidden * (root_coef + (root_coef * cube_coef) * square))
    half_up = 0.5 + 0.5 * tanh_val
    active = hidden * half_up
    derivative = half_up + active * (1.0 - half_up) * (
        2.0 * root_coef + (6.0 * root_coef * cube_coef) * square
    )
    return active, derivative


def steps(extent, most):
    size = min(extent, most)
    return [(at, size) for at in range(0, extent, size)]


def stack(refs, part, block):
    return jnp.concatenate([ref[part * block : (part + 1) * block, :] for ref in refs], axis=0)


def slot_rows(routes, keep, combine, me, experts, block, capacity):
    count = routes.shape[1]
    kept = keep > 0
    first, second = routes[0:1, :] ^ me, routes[1:2, :] ^ me
    ids = lax.broadcasted_iota(jnp.int32, (experts, count), 0)
    first_hot = jnp.where(first == ids, 1.0, 0.0)
    second_hot = jnp.where((second == ids) & kept, 1.0, 0.0)
    earlier = jnp.where(
        lax.broadcasted_iota(jnp.int32, (count, count), 0)
        < lax.broadcasted_iota(jnp.int32, (count, count), 1),
        1.0,
        0.0,
    ).astype(bf16)
    first_pos = dot(first_hot.astype(bf16), earlier)
    second_pos = dot(second_hot.astype(bf16), earlier) + jnp.sum(first_hot, axis=1, keepdims=True)
    first_slot = jnp.sum(first_pos * first_hot, axis=0, keepdims=True)
    second_slot = jnp.sum(second_pos * second_hot, axis=0, keepdims=True)
    first_flat = jnp.where(first_slot < capacity, first.astype(f32) * block + first_slot, -1.0)
    second_flat = jnp.where(
        kept & (second_slot < capacity), second.astype(f32) * block + second_slot, -1.0
    )
    weights = combine.astype(f32)
    return first_flat, second_flat, weights[0:1, :], weights[1:2, :]


def picks(first_flat, second_flat, rows):
    ids = lax.broadcasted_iota(jnp.int32, (rows, first_flat.shape[1]), 0)
    return ids == first_flat.astype(jnp.int32), ids == second_flat.astype(jnp.int32)


def place(pick, source, out_refs, block):
    for at, size in steps(source.shape[1], 256):
        rows = dot(pick, source[:, at : at + size]).astype(bf16)
        for k, out in enumerate(out_refs):
            out[:, at : at + size] = rows[k * block : (k + 1) * block]


def own_send_kernel(
    experts, block, capacity, routes, keep, combine, tokens, grad_out, meta, *refs
):
    outs, weighted = refs[:experts], refs[experts]

    @pl.when(pl.program_id(0) == 0)
    def _():
        me = lax.axis_index("expert")
        a, b, c, d = slot_rows(
            routes[...], keep[...], combine[...], me, experts, block, capacity
        )
        meta[0:1, :] = a
        meta[1:2, :] = b
        meta[2:3, :] = c
        meta[3:4, :] = d
        meta[4:8, :] = jnp.zeros((4, a.shape[1]), f32)
        first, second = picks(a, b, experts * block)
        weighted[...] = jnp.where(first, c, jnp.where(second, d, 0.0)).astype(bf16)
        chosen = jnp.where(first | second, 1.0, 0.0).astype(bf16)
        place(chosen, tokens, outs, block)

    @pl.when(pl.program_id(0) == 1)
    def _():
        place(weighted[...], grad_out, outs, block)


def send_x_kernel(experts, block, meta, tokens, *outs):
    first, second = picks(meta[0:1, :], meta[1:2, :], experts * block)
    place(jnp.where(first | second, 1.0, 0.0).astype(bf16), tokens, outs, block)


def send_s_kernel(experts, block, meta, grad_out, *outs):
    first, second = picks(meta[0:1, :], meta[1:2, :], experts * block)
    weighted = jnp.where(first, meta[2:3, :], jnp.where(second, meta[3:4, :], 0.0)).astype(bf16)
    place(weighted, grad_out, outs, block)


def add_tokens(grad, w_in, total, gates, outs, block, capacity):
    step, last = pl.program_id(0), pl.num_programs(0) - 1
    more = dot(grad, w_in, TN)

    @pl.when(step == 0)
    def _():
        total[...] = more

    @pl.when((step > 0) & (step < last))
    def _():
        total[...] += more

    @pl.when(step == last)
    def _():
        rows = (total[...] + more).astype(bf16)
        gate_rows = gates[0:1, :].astype(bf16)
        for k, out in enumerate(outs):
            out[...] = rows[k * block : (k + 1) * block]
            out[capacity : capacity + 1, 0:block] = gate_rows[:, k * block : (k + 1) * block]


def add_gates(active, up, gates):
    more = jnp.sum(active.astype(f32) * up, axis=0, keepdims=True)

    @pl.when(pl.program_id(0) == 0)
    def _():
        gates[0:1, :] = more

    @pl.when(pl.program_id(0) > 0)
    def _():
        gates[0:1, :] += more


def own_expert_kernel(experts, block, capacity, pos, w_in, w_out, *refs):
    blocks, (act, grad), outs = refs[:experts], refs[experts : experts + 2], refs[experts + 2 : -2]
    total, gates = refs[-2:]
    x, s = stack(blocks, 0, block), stack(blocks, 1, block)
    active, slope = gelu_slope(dot(w_in[0], x, NT))
    active = active.astype(bf16)
    act[...] = active
    up = dot(w_out[0], s, NT)
    add_gates(active, up, gates)
    hidden_grad = (up * slope).astype(bf16)
    grad[...] = hidden_grad
    add_tokens(hidden_grad, w_in[0], total, gates, outs, block, capacity)


def act_kernel(experts, block, pos, w_in, *refs):
    blocks, (act, slope) = refs[:experts], refs[experts:]
    active, derivative = gelu_slope(dot(w_in[0], stack(blocks, 0, block), NT))
    act[...] = active.astype(bf16)
    slope[...] = derivative.astype(bf16)


def grad_kernel(experts, block, capacity, pos, w_in, w_out, act, slope, *refs):
    blocks, grad, outs = refs[:experts], refs[experts], refs[experts + 1 : -2]
    total, gates = refs[-2:]
    up = dot(w_out[0], stack(blocks, 0, block), NT)
    add_gates(act[...], up, gates)
    hidden_grad = (up * slope[...].astype(f32)).astype(bf16)
    grad[...] = hidden_grad
    add_tokens(hidden_grad, w_in[0], total, gates, outs, block, capacity)


def outer_rows(own_ref, other_ref, own_rows, other_rows, at, size):
    return dot(own_ref[pl.ds(at, size), :], own_rows) + dot(other_ref[pl.ds(at, size), :], other_rows)


def away_kernel(experts, block, owners, pos, own, other, *refs):
    own_blocks, other_blocks, outs = refs[:experts], refs[experts : 2 * experts], refs[2 * experts :]
    own_rows, other_rows = stack(own_blocks, 0, block), stack(other_blocks, 0, block)
    size = own.shape[0] // owners
    for r, out in enumerate(outs):
        at = pl.multiple_of(lax.rem(pos[1] + r + 1, owners) * size, size)
        out[...] = outer_rows(own, other, own_rows, other_rows, at, size).astype(bf16)


def home_kernel(experts, block, owners, pos, own, other, *refs):
    own_blocks, other_blocks = refs[:experts], refs[experts : 2 * experts]
    got, out = refs[2 * experts : 2 * experts + owners - 1], refs[-1]
    own_rows, other_rows = stack(own_blocks, 0, block), stack(other_blocks, 0, block)
    size = own.shape[0] // owners
    at = pl.multiple_of(pos[1] * size, size)
    total = outer_rows(own, other, own_rows, other_rows, at, size)
    for ref in got:
        total = total + ref[...].astype(f32)
    out[0] = total


def gathered(meta, refs, experts, block):
    first, second = picks(meta[0:1, :], meta[1:2, :], experts * block)
    chosen = jnp.where(first | second, 1.0, 0.0).astype(bf16)
    return dot(chosen, stack(refs, 0, block), TN)


def gate_rows(meta, refs, block, capacity):
    values = jnp.concatenate([ref[capacity : capacity + 1, 0:block] for ref in refs], axis=0)
    out = []
    for at in (0, 1):
        flat = meta[at : at + 1, :].astype(jnp.int32)
        live = flat >= 0
        which = jnp.where(live, flat, 0) // block
        where = flat - which * block
        lane = lax.broadcasted_iota(jnp.int32, (block, flat.shape[1]), 0)
        hit = jnp.where((lane == where) & live, 1.0, 0.0).astype(bf16)
        by_block = dot(values, hit)
        mine = lax.broadcasted_iota(jnp.int32, by_block.shape, 0) == which
        gate = jnp.sum(jnp.where(mine, by_block, 0.0), axis=0, keepdims=True)
        out.append(jnp.where(live, gate / meta[at + 2 : at + 3, :], 0.0))
    return out


def other_collect_kernel(experts, block, capacity, meta, *refs):
    blocks, (out, gates) = refs[:experts], refs[experts:]
    out[...] = gathered(meta, blocks, experts, block).astype(bf16)

    @pl.when(pl.program_id(0) == 0)
    def _():
        first, second = gate_rows(meta, blocks, block, capacity)
        gates[0:1, :] = first
        gates[1:2, :] = second
        gates[2:8, :] = jnp.zeros((6, first.shape[1]), f32)


def own_collect_kernel(experts, block, capacity, meta, got, got_gates, *refs):
    blocks, (grad_tokens, grad_combine) = refs[:experts], refs[experts:]
    tokens = gathered(meta, blocks, experts, block)
    grad_tokens[...] = (tokens + got[...].astype(f32)).astype(bf16)

    @pl.when(pl.program_id(0) == 0)
    def _():
        gates = gate_rows(meta, blocks, block, capacity)
        grad_combine[...] = (jnp.concatenate(gates, axis=0) + got_gates[0:2, :]).astype(bf16)


def shaped(shape, dtype=bf16):
    return jax.ShapeDtypeStruct(shape, dtype)


def full(array):
    return pl.BlockSpec(array.shape, lambda g, *pos, rank=array.ndim: (0,) * rank)


def columns(array, parts, first=0):
    size = array.shape[-1] // parts
    lead = array.shape[:-1]
    return pl.BlockSpec(
        lead + (size,), lambda g, *pos, rank=array.ndim: (0,) * (rank - 1) + (first + g,)
    )


def rows(array, size):
    return pl.BlockSpec((size, array.shape[1]), lambda g, *pos: (g, 0))


def half_rows(array, parts):
    size = array.shape[1] // 2 // parts
    return pl.BlockSpec((1, size, array.shape[2]), lambda g, pos: (0, pos[0] * parts + g, 0))


def call(kernel, grid, scalars, operands, results, scratch=(), flops=0, alias=None):
    arrays, in_specs = [a for a, _ in operands], [s for _, s in operands]
    outs, out_specs = [a for a, _ in results], [s for _, s in results]
    moved = sum(a.size * a.dtype.itemsize for a in arrays + outs)
    return pl.pallas_call(
        kernel,
        out_shape=outs,
        grid_spec=pltpu.PrefetchScalarGridSpec(
            num_scalar_prefetch=len(scalars),
            grid=(grid,),
            in_specs=in_specs,
            out_specs=out_specs,
            scratch_shapes=list(scratch),
        ),
        input_output_aliases=alias or {},
        compiler_params=pltpu.CompilerParams(vmem_limit_bytes=28 << 20),
        cost_estimate=pl.CostEstimate(flops=int(flops), transcendentals=0, bytes_accessed=moved),
    )(*scalars, *arrays)


def part_of(array, part, block, parts, first=0):
    return pl.BlockSpec((block, array.shape[1] // parts), lambda g, *pos: (part, first + g))


def per_device(tokens, grad_out, routes, keep_second, combine, w_in, w_out):
    experts, planes = lax.axis_size("expert"), lax.axis_size("dp")
    count, width = tokens.shape
    capacity = 5 * count // (2 * experts)
    block = -(-(capacity + 1) // 16) * 16
    owners = planes // 2
    units = w_in.shape[1] // 2
    share = units // owners
    slots = experts * block
    if planes % 2 or experts & (experts - 1):
        raise ValueError("mesh sizes")
    plane = lax.axis_index("dp")
    pos = jnp.stack([plane // owners, plane % owners]).astype(jnp.int32)
    bind = functools.partial

    def across(value):
        return lax.ppermute(value, "dp", [(j, (j + owners) % planes) for j in range(planes)])

    def exchange(values):
        return [values[0]] + [
            lax.ppermute(values[k], "expert", [(i, i ^ k) for i in range(experts)])
            for k in range(1, experts)
        ]

    def to_owners(values):
        return [
            lax.ppermute(
                value,
                "dp",
                [(j, j // owners * owners + (j + r + 1) % owners) for j in range(planes)],
            )
            for r, value in enumerate(values)
        ]

    def each(arrays, spec, *more):
        return [(a, spec(a, *more)) for a in arrays]

    routes_t, keep_t, combine_t = routes.T, keep_second.reshape(1, count), combine.T

    def stay(array):
        return pltpu.with_memory_space_constraint(array, pltpu.HBM)

    w_in, w_out = stay(w_in), stay(w_out)
    other_x = across(tokens)
    other_dy = across(grad_out)
    blocks2 = [shaped((2 * block, width))] * experts
    blocks1 = [shaped((block, width))] * experts
    act_shape = shaped((units, slots))
    unit_parts = max(units // 256, 1)
    unit_rows = units // unit_parts
    sums = [pltpu.VMEM((slots, width), f32), pltpu.VMEM((8, slots), f32)]
    meta_shape = shaped((8, count), f32)
    meta, *own_blocks = call(
        bind(own_send_kernel, experts, block, capacity),
        2,
        [],
        each([stay(a) for a in (routes_t, keep_t, combine_t, tokens, grad_out)], full),
        each([meta_shape], full) + each(blocks2, rows, block),
        [pltpu.VMEM((slots, count), bf16)],
        4 * slots * count * width,
    )
    own_blocks = exchange(own_blocks)
    other_meta = across(meta)
    other_xb = call(
        bind(send_x_kernel, experts, block),
        2,
        [],
        each([other_meta], full) + each([other_x], columns, 2),
        each(blocks1, columns, 2),
        flops=2 * slots * count * width,
    )
    other_xb = exchange(other_xb)
    other_sb = call(
        bind(send_s_kernel, experts, block),
        2,
        [],
        each([other_meta], full) + each([other_dy], columns, 2),
        each(blocks1, columns, 2),
        flops=2 * slots * count * width,
    )
    other_sb = exchange(other_sb)
    own_act, own_grad, *own_back = call(
        bind(own_expert_kernel, experts, block, capacity),
        unit_parts,
        [pos],
        each([w_in, w_out], half_rows, unit_parts) + each(own_blocks, full),
        each([act_shape] * 2, rows, unit_rows) + each(blocks1, full),
        sums,
        6 * slots * units * width,
    )
    other_act, other_slope = call(
        bind(act_kernel, experts, block),
        unit_parts,
        [pos],
        each([w_in], half_rows, unit_parts) + each(other_xb, full),
        each([act_shape] * 2, rows, unit_rows),
        flops=2 * slots * units * width,
    )
    runs = 4
    fed = slots * share * width

    def away(acts, left, part, right, first, many):
        extent = width // runs * many
        return call(
            bind(away_kernel, experts, block, owners),
            many,
            [pos],
            each(acts, full)
            + each(left, part_of, part, block, runs, first)
            + each(right, part_of, 0, block, runs, first),
            each([shaped((share, extent))] * (owners - 1), columns, many),
            flops=4 * fed * (owners - 1) * many // runs,
        )

    def home(acts, left, part, right, got, first, many, into=None):
        goal = shaped((1, share, width), f32)
        operands = (
            each(acts, full)
            + each(left, part_of, part, block, runs, first)
            + each(right, part_of, 0, block, runs, first)
            + each(got, columns, many)
        )
        alias = None
        if into is not None:
            operands.append((into, pl.BlockSpec(memory_space=pl.ANY)))
            alias = {len(operands): 0}
        return call(
            bind(home_kernel, experts, block, owners),
            many,
            [pos],
            operands,
            each([goal], columns, runs, first),
            flops=4 * fed * many // runs,
            alias=alias,
        )[0]

    away_out = away([own_act, other_act], own_blocks, 1, other_sb, 0, runs)
    got_out = to_owners(away_out)
    other_grad, *other_back = call(
        bind(grad_kernel, experts, block, capacity),
        unit_parts,
        [pos],
        each([w_in, w_out], half_rows, unit_parts)
        + each([other_act, other_slope], rows, unit_rows)
        + each(other_sb, full),
        each([act_shape], rows, unit_rows) + each(blocks1, full),
        sums,
        4 * slots * units * width,
    )
    other_back = exchange(other_back)
    in_args = [own_grad, other_grad], own_blocks, 0, other_xb
    away_a = away(*in_args, 0, 3)
    got_a = to_owners(away_a)
    away_b = away(*in_args, 3, 1)
    got_b = to_owners(away_b)
    own_back = exchange(own_back)
    other_part, other_gates = call(
        bind(other_collect_kernel, experts, block, capacity),
        2,
        [],
        each([other_meta], full) + each(other_back, columns, 2),
        each([shaped((count, width))], columns, 2) + each([meta_shape], full),
        flops=2 * slots * count * width,
    )
    part = across(other_part)
    part_gates = across(other_gates)
    grad_outw = home([own_act, other_act], own_blocks, 1, other_sb, got_out, 0, runs)
    grad_tokens, grad_combine = call(
        bind(own_collect_kernel, experts, block, capacity),
        2,
        [],
        each([meta], full)
        + each([part], columns, 2)
        + each([part_gates], full)
        + each(own_back, columns, 2),
        each([shaped((count, width))], columns, 2) + each([shaped((2, count))], full),
        flops=2 * slots * count * width,
    )
    grad_in = home(*in_args, got_a, 0, 3)
    grad_in = home(*in_args, got_b, 3, 1, grad_in)
    return grad_tokens, grad_combine.T, grad_in, grad_outw


def solution(mesh):
    return jax.shard_map(
        per_device,
        mesh=mesh,
        in_specs=(
            P(("expert", "dp"), None),
            P(("expert", "dp"), None),
            P(("expert", "dp"), None),
            P(("expert", "dp")),
            P(("expert", "dp"), None),
            P("expert", None, None),
            P("expert", None, None),
        ),
        out_specs=(
            P(("expert", "dp"), None),
            P(("expert", "dp"), None),
            P("expert", "dp", None),
            P("expert", "dp", None),
        ),
        check_vma=False,
    )
```

```python
import functools

import jax
import jax.numpy as jnp
from jax import lax
from jax.experimental import pallas as pl
from jax.experimental.pallas import tpu as pltpu
from jax.sharding import PartitionSpec as P


root_coef = 0.7978845608
cube_coef = 0.044715
bf16 = jnp.bfloat16
f32 = jnp.float32

NN = (((1,), (0,)), ((), ()))
NT = (((1,), (1,)), ((), ()))
TN = (((0,), (0,)), ((), ()))


def dot(a, b, dims=NN):
    return lax.dot_general(a, b, dims, preferred_element_type=f32)


def gelu_slope(hidden):
    square = hidden * hidden
    tanh_val = jnp.tanh(hidden * (root_coef + (root_coef * cube_coef) * square))
    half_up = 0.5 + 0.5 * tanh_val
    active = hidden * half_up
    derivative = half_up + active * (1.0 - half_up) * (
        2.0 * root_coef + (6.0 * root_coef * cube_coef) * square
    )
    return active, derivative


def steps(extent, most):
    size = min(extent, most)
    return [(at, size) for at in range(0, extent, size)]


def stack(refs, experts):
    runs = [
        jnp.concatenate([ref[...] for ref in refs[at : at + experts]], axis=0)
        for at in range(0, len(refs), experts)
    ]
    return runs[0] if len(runs) == 1 else jnp.concatenate(runs, axis=1)


def slot_rows(routes, keep, combine, me, experts, block, capacity):
    count = routes.shape[1]
    kept = keep > 0
    first, second = routes[0:1, :] ^ me, routes[1:2, :] ^ me
    ids = lax.broadcasted_iota(jnp.int32, (experts, count), 0)
    first_hot = jnp.where(first == ids, 1.0, 0.0)
    second_hot = jnp.where((second == ids) & kept, 1.0, 0.0)
    earlier = jnp.where(
        lax.broadcasted_iota(jnp.int32, (count, count), 0)
        < lax.broadcasted_iota(jnp.int32, (count, count), 1),
        1.0,
        0.0,
    ).astype(bf16)
    first_pos = dot(first_hot.astype(bf16), earlier)
    second_pos = dot(second_hot.astype(bf16), earlier) + jnp.sum(first_hot, axis=1, keepdims=True)
    first_slot = jnp.sum(first_pos * first_hot, axis=0, keepdims=True)
    second_slot = jnp.sum(second_pos * second_hot, axis=0, keepdims=True)
    first_flat = jnp.where(first_slot < capacity, first.astype(f32) * block + first_slot, -1.0)
    second_flat = jnp.where(
        kept & (second_slot < capacity), second.astype(f32) * block + second_slot, -1.0
    )
    weights = combine.astype(f32)
    return first_flat, second_flat, weights[0:1, :], weights[1:2, :]


def picks(first_flat, second_flat, rows):
    ids = lax.broadcasted_iota(jnp.int32, (rows, first_flat.shape[1]), 0)
    return ids == first_flat.astype(jnp.int32), ids == second_flat.astype(jnp.int32)


def place(pick, source, out_refs, block, left=0):
    for at, size in steps(source.shape[1], 256):
        rows = dot(pick, source[:, at : at + size]).astype(bf16)
        for k, out in enumerate(out_refs):
            out[:, left + at : left + at + size] = rows[k * block : (k + 1) * block]


def own_send_kernel(experts, block, capacity, routes, keep, combine, tokens, grad_out, meta, *outs):
    me = lax.axis_index("expert")
    a, b, c, d = slot_rows(routes[...], keep[...], combine[...], me, experts, block, capacity)
    meta[0:1, :] = a
    meta[1:2, :] = b
    meta[2:3, :] = c
    meta[3:4, :] = d
    meta[4:8, :] = jnp.zeros((4, a.shape[1]), f32)
    first, second = picks(a, b, experts * block)
    place(jnp.where(first | second, 1.0, 0.0).astype(bf16), tokens, outs, block)
    weighted = jnp.where(first, c, jnp.where(second, d, 0.0)).astype(bf16)
    place(weighted, grad_out, outs, block, tokens.shape[1])


def load_kernel(pos, w_in, w_out, in_half, out_half):
    in_half[...] = w_in[0]
    out_half[...] = w_out[0]


def send_x_kernel(experts, block, meta, tokens, *outs):
    first, second = picks(meta[0:1, :], meta[1:2, :], experts * block)
    place(jnp.where(first | second, 1.0, 0.0).astype(bf16), tokens, outs, block)


def send_s_kernel(experts, block, meta, grad_out, *outs):
    first, second = picks(meta[0:1, :], meta[1:2, :], experts * block)
    weighted = jnp.where(first, meta[2:3, :], jnp.where(second, meta[3:4, :], 0.0))
    place(weighted.astype(bf16), grad_out, outs, block)


def add_tokens(grad, w_in, total, gates, outs, block, capacity):
    step, last = pl.program_id(0), pl.num_programs(0) - 1
    more = dot(grad, w_in, TN)

    @pl.when(step == 0)
    def _():
        total[...] = more

    @pl.when((step > 0) & (step < last))
    def _():
        total[...] += more

    @pl.when(step == last)
    def _():
        rows = (total[...] + more).astype(bf16)
        gate_rows = gates[0:1, :].astype(bf16)
        for k, out in enumerate(outs):
            out[...] = rows[k * block : (k + 1) * block]
            out[capacity : capacity + 1, 0:block] = gate_rows[:, k * block : (k + 1) * block]


def add_gates(active, up, gates):
    more = jnp.sum(active.astype(f32) * up, axis=0, keepdims=True)

    @pl.when(pl.program_id(0) == 0)
    def _():
        gates[0:1, :] = more

    @pl.when(pl.program_id(0) > 0)
    def _():
        gates[0:1, :] += more


def act_kernel(experts, w_in, *refs):
    blocks, (act, slope) = refs[:-2], refs[-2:]
    active, derivative = gelu_slope(dot(w_in[...], stack(blocks, experts), NT))
    act[...] = active.astype(bf16)
    slope[...] = derivative.astype(bf16)


def grad_kernel(experts, block, capacity, w_in, w_out, act, slope, *refs):
    (total, gates), outs = refs[-2:], refs[-2 - experts : -2]
    grad, blocks = refs[-3 - experts], refs[: -3 - experts]
    up = dot(w_out[...], stack(blocks, experts), NT)
    add_gates(act[...], up, gates)
    hidden_grad = (up * slope[...].astype(f32)).astype(bf16)
    grad[...] = hidden_grad
    add_tokens(hidden_grad, w_in[...], total, gates, outs, block, capacity)


def outer_rows(own_ref, other_ref, own_rows, other_rows, at, size):
    return dot(own_ref[pl.ds(at, size), :], own_rows) + dot(other_ref[pl.ds(at, size), :], other_rows)


def away_kernel(experts, owners, pos, own, other, *refs):
    own_blocks, other_blocks, outs = refs[:experts], refs[experts : 2 * experts], refs[2 * experts :]
    own_rows, other_rows = stack(own_blocks, experts), stack(other_blocks, experts)
    size = own.shape[0] // owners
    for r, out in enumerate(outs):
        at = pl.multiple_of(lax.rem(pos[1] + r + 1, owners) * size, size)
        out[...] = outer_rows(own, other, own_rows, other_rows, at, size).astype(bf16)


def home_kernel(experts, owners, pos, own, other, *refs):
    own_blocks, other_blocks = refs[:experts], refs[experts : 2 * experts]
    got, out = refs[2 * experts : 2 * experts + owners - 1], refs[-1]
    size = own.shape[0] // owners
    at = pl.multiple_of(pos[1] * size, size)
    total = outer_rows(
        own, other, stack(own_blocks, experts), stack(other_blocks, experts), at, size
    )
    for ref in got:
        total = total + ref[...].astype(f32)
    out[0] = total


def before_kernel(experts, owners, pos, own, other, *refs):
    own_blocks, other_blocks, out = refs[:experts], refs[experts : 2 * experts], refs[-1]
    size = own.shape[0] // owners
    at = pl.multiple_of(pos[1] * size, size)
    out[...] = outer_rows(
        own, other, stack(own_blocks, experts), stack(other_blocks, experts), at, size
    )


def after_kernel(owners, before, *refs):
    total = before[...]
    for ref in refs[: owners - 1]:
        total = total + ref[...].astype(f32)
    refs[-1][0] = total


def gathered(meta, refs, experts, block):
    first, second = picks(meta[0:1, :], meta[1:2, :], experts * block)
    chosen = jnp.where(first | second, 1.0, 0.0).astype(bf16)
    return dot(chosen, stack(refs, experts), TN)


def gate_rows(meta, refs, block, capacity):
    values = jnp.concatenate([ref[capacity : capacity + 1, 0:block] for ref in refs], axis=0)
    out = []
    for at in (0, 1):
        flat = meta[at : at + 1, :].astype(jnp.int32)
        live = flat >= 0
        which = jnp.where(live, flat, 0) // block
        where = flat - which * block
        lane = lax.broadcasted_iota(jnp.int32, (block, flat.shape[1]), 0)
        hit = jnp.where((lane == where) & live, 1.0, 0.0).astype(bf16)
        by_block = dot(values, hit)
        mine = lax.broadcasted_iota(jnp.int32, by_block.shape, 0) == which
        gate = jnp.sum(jnp.where(mine, by_block, 0.0), axis=0, keepdims=True)
        out.append(jnp.where(live, gate / meta[at + 2 : at + 3, :], 0.0))
    return out


def collect_kernel(experts, block, capacity, meta, *refs):
    blocks, (out, gates) = refs[:experts], refs[experts:]
    out[...] = gathered(meta, blocks, experts, block).astype(out.dtype)

    @pl.when(pl.program_id(0) == 0)
    def _():
        first, second = gate_rows(meta, blocks, block, capacity)
        gates[0:1, :] = first
        gates[1:2, :] = second
        gates[2:8, :] = jnp.zeros((6, first.shape[1]), f32)


def join_kernel(own, own_gates, got, got_gates, grad_tokens, grad_combine):
    grad_tokens[...] = (own[...] + got[...].astype(f32)).astype(bf16)
    grad_combine[...] = (own_gates[0:2, :] + got_gates[0:2, :]).astype(bf16)


def shaped(shape, dtype=bf16):
    return jax.ShapeDtypeStruct(shape, dtype)


def full(array):
    return pl.BlockSpec(array.shape, lambda g, *pos, rank=array.ndim: (0,) * rank)


def columns(array, parts, first=0):
    size = array.shape[-1] // parts
    lead = array.shape[:-1]
    return pl.BlockSpec(
        lead + (size,), lambda g, *pos, rank=array.ndim: (0,) * (rank - 1) + (first + g,)
    )


def rows(array, size):
    return pl.BlockSpec((size, array.shape[1]), lambda g, *pos: (g, 0))


def half_rows(array, parts):
    size = array.shape[1] // 2 // parts
    return pl.BlockSpec((1, size, array.shape[2]), lambda g, pos: (0, pos[0] * parts + g, 0))


def call(kernel, grid, scalars, operands, results, scratch=(), flops=0, alias=None):
    arrays, in_specs = [a for a, _ in operands], [s for _, s in operands]
    outs, out_specs = [a for a, _ in results], [s for _, s in results]
    moved = sum(a.size * a.dtype.itemsize for a in arrays + outs)
    return pl.pallas_call(
        kernel,
        out_shape=outs,
        grid_spec=pltpu.PrefetchScalarGridSpec(
            num_scalar_prefetch=len(scalars),
            grid=(grid,),
            in_specs=in_specs,
            out_specs=out_specs,
            scratch_shapes=list(scratch),
        ),
        input_output_aliases=alias or {},
        compiler_params=pltpu.CompilerParams(vmem_limit_bytes=28 << 20),
        cost_estimate=pl.CostEstimate(flops=int(flops), transcendentals=0, bytes_accessed=moved),
    )(*scalars, *arrays)


def window(arrays, start, size):
    return [
        (a, pl.BlockSpec((a.shape[0], size), lambda g, *pos: (0, start // size))) for a in arrays
    ]


def runs_of(arrays, start, run):
    return [
        (a, pl.BlockSpec((a.shape[0], run), lambda g, *pos: (0, start // run + g))) for a in arrays
    ]


def per_device(tokens, grad_out, routes, keep_second, combine, w_in, w_out):
    experts, planes = lax.axis_size("expert"), lax.axis_size("dp")
    count, width = tokens.shape
    capacity = 5 * count // (2 * experts)
    block = -(-(capacity + 1) // 16) * 16
    owners = planes // 2
    units = w_in.shape[1] // 2
    share = units // owners
    slots = experts * block
    if planes % 2 or experts & (experts - 1):
        raise ValueError("mesh sizes")
    plane = lax.axis_index("dp")
    pos = jnp.stack([plane // owners, plane % owners]).astype(jnp.int32)
    bind = functools.partial

    def across(value):
        return lax.ppermute(value, "dp", [(j, (j + owners) % planes) for j in range(planes)])

    def exchange(values):
        return [values[0]] + [
            lax.ppermute(values[k], "expert", [(i, i ^ k) for i in range(experts)])
            for k in range(1, experts)
        ]

    def to_owners(values):
        return [
            lax.ppermute(
                value,
                "dp",
                [(j, j // owners * owners + (j + r + 1) % owners) for j in range(planes)],
            )
            for r, value in enumerate(values)
        ]

    def each(arrays, spec, *more):
        return [(a, spec(a, *more)) for a in arrays]

    routes_t, keep_t, combine_t = routes.T, keep_second.reshape(1, count), combine.T

    def stay(array):
        return pltpu.with_memory_space_constraint(array, pltpu.HBM)

    other_x = across(tokens)
    half = width // 2
    other_dya = across(grad_out[:, :half])
    other_dyb = across(grad_out[:, half:])

    def blocks(columns_of):
        return [shaped((block, columns_of))] * experts

    act_shape = shaped((units, slots))
    unit_parts = max(units // 256, 1)
    unit_rows = units // unit_parts
    sums = [pltpu.VMEM((slots, width), f32), pltpu.VMEM((8, slots), f32)]
    meta_shape = shaped((8, count), f32)
    meta, *own_xs = call(
        bind(own_send_kernel, experts, block, capacity),
        1,
        [],
        each([stay(a) for a in (routes_t, keep_t, combine_t, tokens, grad_out)], full),
        each([meta_shape] + blocks(2 * width), full),
        flops=4 * slots * count * width,
    )
    own_xs = exchange(own_xs)
    half_in, half_out = call(
        load_kernel,
        4,
        [pos],
        each([stay(w_in), stay(w_out)], half_rows, 4),
        each([shaped((units, width))] * 2, rows, units // 4),
    )
    other_meta = across(meta)
    other_xb = call(
        bind(send_x_kernel, experts, block),
        2,
        [],
        each([other_meta], full) + each([other_x], columns, 2),
        each(blocks(width), columns, 2),
        flops=2 * slots * count * width,
    )
    x_out = exchange(other_xb)
    sent = []
    for values in (other_dya, other_dyb):
        out = call(
            bind(send_s_kernel, experts, block),
            1,
            [],
            each([other_meta, values], full),
            each(blocks(half), full),
            flops=slots * count * width,
        )
        sent.append(exchange(out))
    own_x, other_x = (own_xs, 0), (x_out, 0)
    own_sa, other_sa = (own_xs, width), (sent[0], 0)
    own_sb, other_sb = (own_xs, width + half), (sent[1], 0)

    def act(x):
        return call(
            bind(act_kernel, experts),
            unit_parts,
            [],
            each([half_in], rows, unit_rows) + window(*x, width),
            each([act_shape] * 2, rows, unit_rows),
            flops=2 * slots * units * width,
        )

    def grad(acts, sa, sb):
        result, *back = call(
            bind(grad_kernel, experts, block, capacity),
            unit_parts,
            [],
            each([half_in, half_out], rows, unit_rows)
            + each(acts, rows, unit_rows)
            + window(*sa, half)
            + window(*sb, half),
            each([act_shape], rows, unit_rows) + each(blocks(width), full),
            sums,
            4 * slots * units * width,
        )
        return result, back

    own_act, own_slope = act(own_x)
    other_act, other_slope = act(other_x)
    run = width // 4
    fed = slots * share * run

    def away(acts, left, right, first, many):
        return call(
            bind(away_kernel, experts, owners),
            many,
            [pos],
            each(acts, full)
            + runs_of(left[0], left[1] + first * run, run)
            + runs_of(right[0], right[1] + first * run, run),
            each([shaped((share, many * run))] * (owners - 1), columns, many),
            flops=4 * fed * (owners - 1) * many,
        )

    goal = shaped((1, share, width), f32)

    def into(array, operands, prefetched):
        if array is None:
            return operands, None
        return operands + [(array, pl.BlockSpec(memory_space=pl.ANY))], {
            len(operands) + prefetched: 0
        }

    def home(acts, left, right, got, first, many, array=None):
        operands, alias = into(
            array,
            each(acts, full)
            + runs_of(*left, run)
            + runs_of(*right, run)
            + each(got, columns, many),
            1,
        )
        return call(
            bind(home_kernel, experts, owners),
            many,
            [pos],
            operands,
            each([goal], columns, 4, first),
            flops=4 * fed * many,
            alias=alias,
        )[0]

    def after(before, got, first, many, array=None):
        operands, alias = into(
            array, runs_of([before], first * run, run) + each(got, columns, many), 0
        )
        return call(
            bind(after_kernel, owners),
            many,
            [],
            operands,
            each([goal], columns, 4, first),
            alias=alias,
        )[0]

    out_acts = [own_act, other_act]
    away_oa = away(out_acts, own_sa, other_sa, 0, 2)
    got_oa = to_owners(away_oa)
    away_ob = away(out_acts, own_sb, other_sb, 0, 2)
    got_ob = to_owners(away_ob)
    other_grad, other_back = grad([other_act, other_slope], other_sa, other_sb)
    other_back = exchange(other_back)
    own_grad, own_back = grad([own_act, own_slope], own_sa, own_sb)
    in_acts = [own_grad, other_grad]
    away_a = away(in_acts, own_x, other_x, 0, 3)
    got_a = to_owners(away_a)
    away_b = away(in_acts, own_x, other_x, 3, 1)
    got_b = to_owners(away_b)
    own_back = exchange(own_back)

    def collect(rows_of, back, kind):
        return call(
            bind(collect_kernel, experts, block, capacity),
            2,
            [],
            each([rows_of], full) + each(back, columns, 2),
            each([shaped((count, width), kind)], columns, 2) + each([meta_shape], full),
            flops=2 * slots * count * width,
        )

    other_part, other_gates = collect(other_meta, other_back, bf16)
    part = across(other_part)
    part_gates = across(other_gates)
    grad_outw = home(out_acts, own_sa, other_sa, got_oa, 0, 2)
    grad_outw = home(out_acts, own_sb, other_sb, got_ob, 2, 2, grad_outw)
    own_part, own_gates = collect(meta, own_back, f32)
    before = call(
        bind(before_kernel, experts, owners),
        4,
        [pos],
        each(in_acts, full) + runs_of(*own_x, run) + runs_of(*other_x, run),
        each([shaped((share, width), f32)], columns, 4),
        flops=16 * fed,
    )[0]
    grad_tokens, grad_combine = call(
        join_kernel,
        1,
        [],
        each([own_part, own_gates, part, part_gates], full),
        each([shaped((count, width)), shaped((2, count))], full),
    )
    grad_in = after(before, got_a, 0, 3)
    grad_in = after(before, got_b, 3, 1, grad_in)
    return grad_tokens, grad_combine.T, grad_in, grad_outw


def solution(mesh):
    return jax.shard_map(
        per_device,
        mesh=mesh,
        in_specs=(
            P(("expert", "dp"), None),
            P(("expert", "dp"), None),
            P(("expert", "dp"), None),
            P(("expert", "dp")),
            P(("expert", "dp"), None),
            P("expert", None, None),
            P("expert", None, None),
        ),
        out_specs=(
            P(("expert", "dp"), None),
            P(("expert", "dp"), None),
            P("expert", "dp", None),
            P("expert", "dp", None),
        ),
        check_vma=False,
    )
```

```python
import functools

import jax
import jax.numpy as jnp
from jax import lax
from jax.experimental import pallas as pl
from jax.experimental.pallas import tpu as pltpu
from jax.sharding import PartitionSpec as P


root_coef = 0.7978845608
cube_coef = 0.044715
bf16 = jnp.bfloat16
f32 = jnp.float32

NN = (((1,), (0,)), ((), ()))
NT = (((1,), (1,)), ((), ()))
TN = (((0,), (0,)), ((), ()))


def dot(a, b, dims=NN):
    return lax.dot_general(a, b, dims, preferred_element_type=f32)


def gelu_slope(hidden):
    square = hidden * hidden
    tanh_val = jnp.tanh(hidden * (root_coef + (root_coef * cube_coef) * square))
    half_up = 0.5 + 0.5 * tanh_val
    active = hidden * half_up
    derivative = half_up + active * (1.0 - half_up) * (
        2.0 * root_coef + (6.0 * root_coef * cube_coef) * square
    )
    return active, derivative


def steps(extent, most):
    size = min(extent, most)
    return [(at, size) for at in range(0, extent, size)]


def stack(refs, experts):
    runs = [
        jnp.concatenate([ref[...] for ref in refs[at : at + experts]], axis=0)
        for at in range(0, len(refs), experts)
    ]
    return runs[0] if len(runs) == 1 else jnp.concatenate(runs, axis=1)


def slot_rows(routes, keep, combine, me, experts, block, capacity):
    count = routes.shape[1]
    kept = keep > 0
    first, second = routes[0:1, :] ^ me, routes[1:2, :] ^ me
    ids = lax.broadcasted_iota(jnp.int32, (experts, count), 0)
    first_hot = jnp.where(first == ids, 1.0, 0.0)
    second_hot = jnp.where((second == ids) & kept, 1.0, 0.0)
    earlier = jnp.where(
        lax.broadcasted_iota(jnp.int32, (count, count), 0)
        < lax.broadcasted_iota(jnp.int32, (count, count), 1),
        1.0,
        0.0,
    ).astype(bf16)
    first_pos = dot(first_hot.astype(bf16), earlier)
    second_pos = dot(second_hot.astype(bf16), earlier) + jnp.sum(first_hot, axis=1, keepdims=True)
    first_slot = jnp.sum(first_pos * first_hot, axis=0, keepdims=True)
    second_slot = jnp.sum(second_pos * second_hot, axis=0, keepdims=True)
    first_flat = jnp.where(first_slot < capacity, first.astype(f32) * block + first_slot, -1.0)
    second_flat = jnp.where(
        kept & (second_slot < capacity), second.astype(f32) * block + second_slot, -1.0
    )
    weights = combine.astype(f32)
    return first_flat, second_flat, weights[0:1, :], weights[1:2, :]


def picks(first_flat, second_flat, rows):
    ids = lax.broadcasted_iota(jnp.int32, (rows, first_flat.shape[1]), 0)
    return ids == first_flat.astype(jnp.int32), ids == second_flat.astype(jnp.int32)


def place(pick, source, out_refs, block, left=0):
    for at, size in steps(source.shape[1], 256):
        rows = dot(pick, source[:, at : at + size]).astype(bf16)
        for k, out in enumerate(out_refs):
            out[:, left + at : left + at + size] = rows[k * block : (k + 1) * block]


def own_send_kernel(experts, block, capacity, routes, keep, combine, tokens, grad_out, meta, *outs):
    me = lax.axis_index("expert")
    a, b, c, d = slot_rows(routes[...], keep[...], combine[...], me, experts, block, capacity)
    meta[0:1, :] = a
    meta[1:2, :] = b
    meta[2:3, :] = c
    meta[3:4, :] = d
    meta[4:8, :] = jnp.zeros((4, a.shape[1]), f32)
    first, second = picks(a, b, experts * block)
    place(jnp.where(first | second, 1.0, 0.0).astype(bf16), tokens, outs, block)
    weighted = jnp.where(first, c, jnp.where(second, d, 0.0)).astype(bf16)
    place(weighted, grad_out, outs, block, tokens.shape[1])


def load_kernel(pos, w_in, w_out, in_half, out_half):
    in_half[...] = w_in[0]
    out_half[...] = w_out[0]


def send_x_kernel(experts, block, meta, tokens, *outs):
    first, second = picks(meta[0:1, :], meta[1:2, :], experts * block)
    place(jnp.where(first | second, 1.0, 0.0).astype(bf16), tokens, outs, block)


def send_s_kernel(experts, block, meta, grad_out, *outs):
    first, second = picks(meta[0:1, :], meta[1:2, :], experts * block)
    weighted = jnp.where(first, meta[2:3, :], jnp.where(second, meta[3:4, :], 0.0))
    place(weighted.astype(bf16), grad_out, outs, block)


def accumulate(ref, more):
    @pl.when(pl.program_id(0) == 0)
    def _():
        ref[...] = more

    @pl.when(pl.program_id(0) > 0)
    def _():
        ref[...] += more


def gate_sums(active, up):
    return jnp.sum(active.astype(f32) * up, axis=0, keepdims=True)


def act_kernel(experts, w_in, *refs):
    blocks, (act, slope) = refs[:-2], refs[-2:]
    active, derivative = gelu_slope(dot(w_in[...], stack(blocks, experts), NT))
    act[...] = active.astype(bf16)
    slope[...] = derivative.astype(bf16)


def other_grad_kernel(experts, w_out, slope, *refs):
    up = dot(w_out[...], stack(refs[:-1], experts), NT)
    refs[-1][...] = (up * slope[...].astype(f32)).astype(bf16)


def own_grad_kernel(experts, w_in, w_out, act, slope, *refs):
    blocks, (grad, total, gates) = refs[:-3], refs[-3:]
    up = dot(w_out[...], stack(blocks, experts), NT)
    accumulate(gates, gate_sums(act[...], up))
    hidden_grad = (up * slope[...].astype(f32)).astype(bf16)
    grad[...] = hidden_grad
    accumulate(total, dot(hidden_grad, w_in[...], TN))


def far_kernel(experts, block, capacity, pos, w_in, w_out, near_total, near_gates, *refs):
    x_blocks, s_blocks = refs[:experts], refs[experts : 3 * experts]
    outs, (total, gates) = refs[3 * experts : -2], refs[-2:]
    step, last = pl.program_id(0), pl.num_programs(0) - 1

    @pl.when(step == 0)
    def _():
        total[...] = near_total[...]
        gates[...] = near_gates[...]

    active, slope = gelu_slope(dot(w_in[0], stack(x_blocks, experts), NT))
    up = dot(w_out[0], stack(s_blocks, experts), NT)
    gates[...] += gate_sums(active.astype(bf16), up)
    total[...] += dot((up * slope).astype(bf16), w_in[0], TN)

    @pl.when(step == last)
    def _():
        rows = total[...].astype(bf16)
        gate_rows = gates[...].astype(bf16)
        for k, out in enumerate(outs):
            out[...] = rows[k * block : (k + 1) * block]
            out[capacity : capacity + 1, 0:block] = gate_rows[:, k * block : (k + 1) * block]


def outer_rows(own_ref, other_ref, own_rows, other_rows, at, size):
    return dot(own_ref[pl.ds(at, size), :], own_rows) + dot(other_ref[pl.ds(at, size), :], other_rows)


def away_kernel(experts, owners, pos, own, other, *refs):
    own_blocks, other_blocks, outs = refs[:experts], refs[experts : 2 * experts], refs[2 * experts :]
    own_rows, other_rows = stack(own_blocks, experts), stack(other_blocks, experts)
    size = own.shape[0] // owners
    for r, out in enumerate(outs):
        at = pl.multiple_of(lax.rem(pos[1] + r + 1, owners) * size, size)
        out[...] = outer_rows(own, other, own_rows, other_rows, at, size).astype(bf16)


def home_kernel(experts, owners, pos, own, other, *refs):
    own_blocks, other_blocks = refs[:experts], refs[experts : 2 * experts]
    got, out = refs[2 * experts : 2 * experts + owners - 1], refs[-1]
    size = own.shape[0] // owners
    at = pl.multiple_of(pos[1] * size, size)
    total = outer_rows(
        own, other, stack(own_blocks, experts), stack(other_blocks, experts), at, size
    )
    for ref in got:
        total = total + ref[...].astype(f32)
    out[0] = total


def before_kernel(experts, owners, pos, own, other, *refs):
    own_blocks, other_blocks, out = refs[:experts], refs[experts : 2 * experts], refs[-1]
    size = own.shape[0] // owners
    at = pl.multiple_of(pos[1] * size, size)
    out[...] = outer_rows(
        own, other, stack(own_blocks, experts), stack(other_blocks, experts), at, size
    )


def after_kernel(owners, before, *refs):
    total = before[...]
    for ref in refs[: owners - 1]:
        total = total + ref[...].astype(f32)
    refs[-1][0] = total


def gathered(meta, refs, experts, block):
    first, second = picks(meta[0:1, :], meta[1:2, :], experts * block)
    chosen = jnp.where(first | second, 1.0, 0.0).astype(bf16)
    return dot(chosen, stack(refs, experts), TN)


def gate_rows(meta, refs, block, capacity):
    values = jnp.concatenate([ref[capacity : capacity + 1, 0:block] for ref in refs], axis=0)
    out = []
    for at in (0, 1):
        flat = meta[at : at + 1, :].astype(jnp.int32)
        live = flat >= 0
        which = jnp.where(live, flat, 0) // block
        where = flat - which * block
        lane = lax.broadcasted_iota(jnp.int32, (block, flat.shape[1]), 0)
        hit = jnp.where((lane == where) & live, 1.0, 0.0).astype(bf16)
        by_block = dot(values, hit)
        mine = lax.broadcasted_iota(jnp.int32, by_block.shape, 0) == which
        gate = jnp.sum(jnp.where(mine, by_block, 0.0), axis=0, keepdims=True)
        out.append(jnp.where(live, gate / meta[at + 2 : at + 3, :], 0.0))
    return out


def collect_kernel(experts, block, capacity, meta, *refs):
    blocks, (grad_tokens, grad_combine) = refs[:experts], refs[experts:]
    grad_tokens[...] = gathered(meta, blocks, experts, block).astype(bf16)

    @pl.when(pl.program_id(0) == 0)
    def _():
        gates = gate_rows(meta, blocks, block, capacity)
        grad_combine[...] = jnp.concatenate(gates, axis=0).astype(bf16)


def shaped(shape, dtype=bf16):
    return jax.ShapeDtypeStruct(shape, dtype)


def full(array):
    return pl.BlockSpec(array.shape, lambda g, *pos, rank=array.ndim: (0,) * rank)


def columns(array, parts, first=0):
    size = array.shape[-1] // parts
    lead = array.shape[:-1]
    return pl.BlockSpec(
        lead + (size,), lambda g, *pos, rank=array.ndim: (0,) * (rank - 1) + (first + g,)
    )


def rows(array, size):
    return pl.BlockSpec((size, array.shape[1]), lambda g, *pos: (g, 0))


def half_rows(array, parts, far=0):
    size = array.shape[1] // 2 // parts
    return pl.BlockSpec(
        (1, size, array.shape[2]), lambda g, pos: (0, (pos[0] ^ far) * parts + g, 0)
    )


def call(kernel, grid, scalars, operands, results, scratch=(), flops=0, alias=None):
    arrays, in_specs = [a for a, _ in operands], [s for _, s in operands]
    outs, out_specs = [a for a, _ in results], [s for _, s in results]
    moved = sum(a.size * a.dtype.itemsize for a in arrays + outs)
    return pl.pallas_call(
        kernel,
        out_shape=outs,
        grid_spec=pltpu.PrefetchScalarGridSpec(
            num_scalar_prefetch=len(scalars),
            grid=(grid,),
            in_specs=in_specs,
            out_specs=out_specs,
            scratch_shapes=list(scratch),
        ),
        input_output_aliases=alias or {},
        compiler_params=pltpu.CompilerParams(vmem_limit_bytes=28 << 20),
        cost_estimate=pl.CostEstimate(flops=int(flops), transcendentals=0, bytes_accessed=moved),
    )(*scalars, *arrays)


def window(arrays, start, size):
    return [
        (a, pl.BlockSpec((a.shape[0], size), lambda g, *pos: (0, start // size))) for a in arrays
    ]


def runs_of(arrays, start, run):
    return [
        (a, pl.BlockSpec((a.shape[0], run), lambda g, *pos: (0, start // run + g))) for a in arrays
    ]


def per_device(tokens, grad_out, routes, keep_second, combine, w_in, w_out):
    experts, planes = lax.axis_size("expert"), lax.axis_size("dp")
    count, width = tokens.shape
    capacity = 5 * count // (2 * experts)
    block = -(-(capacity + 1) // 16) * 16
    owners = planes // 2
    units = w_in.shape[1] // 2
    share = units // owners
    slots = experts * block
    if planes % 2 or experts & (experts - 1):
        raise ValueError("mesh sizes")
    plane = lax.axis_index("dp")
    pos = jnp.stack([plane // owners, plane % owners]).astype(jnp.int32)
    bind = functools.partial

    def across(value):
        return lax.ppermute(value, "dp", [(j, (j + owners) % planes) for j in range(planes)])

    def exchange(values):
        return [values[0]] + [
            lax.ppermute(values[k], "expert", [(i, i ^ k) for i in range(experts)])
            for k in range(1, experts)
        ]

    def to_owners(values):
        return [
            lax.ppermute(
                value,
                "dp",
                [(j, j // owners * owners + (j + r + 1) % owners) for j in range(planes)],
            )
            for r, value in enumerate(values)
        ]

    def each(arrays, spec, *more):
        return [(a, spec(a, *more)) for a in arrays]

    routes_t, keep_t, combine_t = routes.T, keep_second.reshape(1, count), combine.T

    def stay(array):
        return pltpu.with_memory_space_constraint(array, pltpu.HBM)

    other_x = across(tokens)
    half = width // 2
    other_dya = across(grad_out[:, :half])
    other_dyb = across(grad_out[:, half:])

    def blocks(columns_of):
        return [shaped((block, columns_of))] * experts

    act_shape = shaped((units, slots))
    unit_parts = max(units // 256, 1)
    unit_rows = units // unit_parts
    meta_shape = shaped((8, count), f32)
    meta, *own_xs = call(
        bind(own_send_kernel, experts, block, capacity),
        1,
        [],
        each([stay(a) for a in (routes_t, keep_t, combine_t, tokens, grad_out)], full),
        each([meta_shape] + blocks(2 * width), full),
        flops=4 * slots * count * width,
    )
    own_xs = exchange(own_xs)
    half_in, half_out = call(
        load_kernel,
        4,
        [pos],
        each([stay(w_in), stay(w_out)], half_rows, 4),
        each([shaped((units, width))] * 2, rows, units // 4),
    )
    other_meta = across(meta)
    other_xb = call(
        bind(send_x_kernel, experts, block),
        2,
        [],
        each([other_meta], full) + each([other_x], columns, 2),
        each(blocks(width), columns, 2),
        flops=2 * slots * count * width,
    )
    x_out = exchange(other_xb)
    sent = []
    for values in (other_dya, other_dyb):
        out = call(
            bind(send_s_kernel, experts, block),
            1,
            [],
            each([other_meta, values], full),
            each(blocks(half), full),
            flops=slots * count * width,
        )
        sent.append(exchange(out))
    own_x, other_x = (own_xs, 0), (x_out, 0)
    own_sa, other_sa = (own_xs, width), (sent[0], 0)
    own_sb, other_sb = (own_xs, width + half), (sent[1], 0)

    def act(x):
        return call(
            bind(act_kernel, experts),
            unit_parts,
            [],
            each([half_in], rows, unit_rows) + window(*x, width),
            each([act_shape] * 2, rows, unit_rows),
            flops=2 * slots * units * width,
        )

    own_act, own_slope = act(own_x)
    other_act, other_slope = act(other_x)
    run = width // 4
    fed = slots * share * run

    def away(acts, left, right, first, many):
        return call(
            bind(away_kernel, experts, owners),
            many,
            [pos],
            each(acts, full)
            + runs_of(left[0], left[1] + first * run, run)
            + runs_of(right[0], right[1] + first * run, run),
            each([shaped((share, many * run))] * (owners - 1), columns, many),
            flops=4 * fed * (owners - 1) * many,
        )

    goal = shaped((1, share, width), f32)

    def into(array, operands, prefetched):
        if array is None:
            return operands, None
        return operands + [(array, pl.BlockSpec(memory_space=pl.ANY))], {
            len(operands) + prefetched: 0
        }

    def home(acts, left, right, got, first, many, array=None):
        operands, alias = into(
            array,
            each(acts, full)
            + runs_of(*left, run)
            + runs_of(*right, run)
            + each(got, columns, many),
            1,
        )
        return call(
            bind(home_kernel, experts, owners),
            many,
            [pos],
            operands,
            each([goal], columns, 4, first),
            flops=4 * fed * many,
            alias=alias,
        )[0]

    def after(before, got, first, many, array=None):
        operands, alias = into(
            array, runs_of([before], first * run, run) + each(got, columns, many), 0
        )
        return call(
            bind(after_kernel, owners),
            many,
            [],
            operands,
            each([goal], columns, 4, first),
            alias=alias,
        )[0]

    out_acts = [own_act, other_act]
    away_oa = away(out_acts, own_sa, other_sa, 0, 2)
    got_oa = to_owners(away_oa)
    away_ob = away(out_acts, own_sb, other_sb, 0, 2)
    got_ob = to_owners(away_ob)
    total_shape, gate_shape = shaped((slots, width), f32), shaped((1, slots), f32)
    own_grad, near_total, near_gates = call(
        bind(own_grad_kernel, experts),
        unit_parts,
        [],
        each([half_in, half_out, own_act, own_slope], rows, unit_rows)
        + window(*own_sa, half)
        + window(*own_sb, half),
        each([act_shape], rows, unit_rows) + each([total_shape, gate_shape], full),
        flops=4 * slots * units * width,
    )
    other_grad = call(
        bind(other_grad_kernel, experts),
        unit_parts,
        [],
        each([half_out, other_slope], rows, unit_rows)
        + window(*other_sa, half)
        + window(*other_sb, half),
        each([act_shape], rows, unit_rows),
        flops=2 * slots * units * width,
    )[0]
    own_back = call(
        bind(far_kernel, experts, block, capacity),
        unit_parts,
        [pos],
        each([stay(w_in), stay(w_out)], half_rows, unit_parts, 1)
        + each([near_total, near_gates], full)
        + window(*own_x, width)
        + window(*own_sa, half)
        + window(*own_sb, half),
        each(blocks(width), full),
        [pltpu.VMEM((slots, width), f32), pltpu.VMEM((1, slots), f32)],
        6 * slots * units * width,
    )
    in_acts = [own_grad, other_grad]
    away_a = away(in_acts, own_x, other_x, 0, 3)
    got_a = to_owners(away_a)
    away_b = away(in_acts, own_x, other_x, 3, 1)
    got_b = to_owners(away_b)
    own_back = exchange(own_back)

    grad_outw = home(out_acts, own_sa, other_sa, got_oa, 0, 2)
    grad_outw = home(out_acts, own_sb, other_sb, got_ob, 2, 2, grad_outw)
    grad_tokens, grad_combine = call(
        bind(collect_kernel, experts, block, capacity),
        2,
        [],
        each([meta], full) + each(own_back, columns, 2),
        each([shaped((count, width))], columns, 2) + each([shaped((2, count))], full),
        flops=2 * slots * count * width,
    )
    before = call(
        bind(before_kernel, experts, owners),
        4,
        [pos],
        each(in_acts, full) + runs_of(*own_x, run) + runs_of(*other_x, run),
        each([shaped((share, width), f32)], columns, 4),
        flops=16 * fed,
    )[0]
    grad_in = after(before, got_a, 0, 3)
    grad_in = after(before, got_b, 3, 1, grad_in)
    return grad_tokens, grad_combine.T, grad_in, grad_outw


def solution(mesh):
    return jax.shard_map(
        per_device,
        mesh=mesh,
        in_specs=(
            P(("expert", "dp"), None),
            P(("expert", "dp"), None),
            P(("expert", "dp"), None),
            P(("expert", "dp")),
            P(("expert", "dp"), None),
            P("expert", None, None),
            P("expert", None, None),
        ),
        out_specs=(
            P(("expert", "dp"), None),
            P(("expert", "dp"), None),
            P("expert", "dp", None),
            P("expert", "dp", None),
        ),
        check_vma=False,
    )
```

```python
import functools

import jax
import jax.numpy as jnp
from jax import lax
from jax.experimental import pallas as pl
from jax.experimental.pallas import tpu as pltpu
from jax.sharding import PartitionSpec as P


root_coef = 0.7978845608
cube_coef = 0.044715
bf16 = jnp.bfloat16
f32 = jnp.float32

NN = (((1,), (0,)), ((), ()))
NT = (((1,), (1,)), ((), ()))
TN = (((0,), (0,)), ((), ()))


def dot(a, b, dims=NN):
    return lax.dot_general(a, b, dims, preferred_element_type=f32)


def gelu_slope(hidden):
    square = hidden * hidden
    tanh_val = jnp.tanh(hidden * (root_coef + (root_coef * cube_coef) * square))
    half_up = 0.5 + 0.5 * tanh_val
    active = hidden * half_up
    derivative = half_up + active * (1.0 - half_up) * (
        2.0 * root_coef + (6.0 * root_coef * cube_coef) * square
    )
    return active, derivative


def steps(extent, most):
    size = min(extent, most)
    return [(at, size) for at in range(0, extent, size)]


def stack(refs, experts):
    runs = [
        jnp.concatenate([ref[...] for ref in refs[at : at + experts]], axis=0)
        for at in range(0, len(refs), experts)
    ]
    return runs[0] if len(runs) == 1 else jnp.concatenate(runs, axis=1)


def slot_rows(routes, keep, combine, me, experts, block, capacity):
    count = routes.shape[1]
    kept = keep > 0
    first, second = routes[0:1, :] ^ me, routes[1:2, :] ^ me
    ids = lax.broadcasted_iota(jnp.int32, (experts, count), 0)
    first_hot = jnp.where(first == ids, 1.0, 0.0)
    second_hot = jnp.where((second == ids) & kept, 1.0, 0.0)
    earlier = jnp.where(
        lax.broadcasted_iota(jnp.int32, (count, count), 0)
        < lax.broadcasted_iota(jnp.int32, (count, count), 1),
        1.0,
        0.0,
    ).astype(bf16)
    first_pos = dot(first_hot.astype(bf16), earlier)
    second_pos = dot(second_hot.astype(bf16), earlier) + jnp.sum(first_hot, axis=1, keepdims=True)
    first_slot = jnp.sum(first_pos * first_hot, axis=0, keepdims=True)
    second_slot = jnp.sum(second_pos * second_hot, axis=0, keepdims=True)
    first_flat = jnp.where(first_slot < capacity, first.astype(f32) * block + first_slot, -1.0)
    second_flat = jnp.where(
        kept & (second_slot < capacity), second.astype(f32) * block + second_slot, -1.0
    )
    weights = combine.astype(f32)
    return first_flat, second_flat, weights[0:1, :], weights[1:2, :]


def picks(first_flat, second_flat, rows):
    ids = lax.broadcasted_iota(jnp.int32, (rows, first_flat.shape[1]), 0)
    return ids == first_flat.astype(jnp.int32), ids == second_flat.astype(jnp.int32)


def place(pick, source, out_refs, block, left=0):
    for at, size in steps(source.shape[1], 256):
        rows = dot(pick, source[:, at : at + size]).astype(bf16)
        for k, out in enumerate(out_refs):
            out[:, left + at : left + at + size] = rows[k * block : (k + 1) * block]


def own_send_kernel(experts, block, capacity, routes, keep, combine, tokens, grad_out, meta, *outs):
    me = lax.axis_index("expert")
    a, b, c, d = slot_rows(routes[...], keep[...], combine[...], me, experts, block, capacity)
    meta[0:1, :] = a
    meta[1:2, :] = b
    meta[2:3, :] = c
    meta[3:4, :] = d
    meta[4:8, :] = jnp.zeros((4, a.shape[1]), f32)
    first, second = picks(a, b, experts * block)
    place(jnp.where(first | second, 1.0, 0.0).astype(bf16), tokens, outs, block)
    weighted = jnp.where(first, c, jnp.where(second, d, 0.0)).astype(bf16)
    place(weighted, grad_out, outs, block, tokens.shape[1])


def load_kernel(pos, w_in, w_out, in_half, out_half):
    in_half[...] = w_in[...]
    out_half[...] = w_out[...]


def send_x_kernel(experts, block, meta, tokens, *outs):
    first, second = picks(meta[0:1, :], meta[1:2, :], experts * block)
    place(jnp.where(first | second, 1.0, 0.0).astype(bf16), tokens, outs, block)


def send_s_kernel(experts, block, meta, grad_out, *refs):
    first, second = picks(meta[0:1, :], meta[1:2, :], experts * block)
    weighted = jnp.where(first, meta[2:3, :], jnp.where(second, meta[3:4, :], 0.0))
    place(weighted.astype(bf16), grad_out, refs[-experts:], block)


def gate_sums(active, up):
    return jnp.sum(active.astype(f32) * up, axis=0, keepdims=True)


def act_rows(weights, x, act, slope, at, size):
    active, derivative = gelu_slope(dot(weights, x, NT))
    act[at : at + size, :] = active.astype(bf16)
    slope[at : at + size, :] = derivative.astype(bf16)


def act_kernel(left, w_in, *refs):
    blocks, (act, slope) = refs[:-2], refs[-2:]
    x = cut(blocks, left, w_in.shape[1])
    for at, size in steps(w_in.shape[0], 256):
        act_rows(w_in[at : at + size, :], x, act, slope, at, size)


def far_act_kernel(experts, pos, w_in, *refs):
    act_rows(w_in[...], stack(refs[:-2], experts), *refs[-2:], 0, w_in.shape[0])


def other_grad_kernel(experts, lefts, w_out, slope, *refs):
    run = w_out.shape[1] // 2
    s = jnp.concatenate(
        [cut(refs[:experts], lefts[0], run), cut(refs[experts : 2 * experts], lefts[1], run)], axis=1
    )
    for at, size in steps(w_out.shape[0], 256):
        up = dot(w_out[at : at + size, :], s, NT)
        refs[-1][at : at + size, :] = (up * slope[at : at + size, :].astype(f32)).astype(bf16)


def own_grad_kernel(experts, lefts, w_in, w_out, act, slope, *refs):
    blocks, (grad, total, gates) = refs[:-3], refs[-3:]
    run = w_out.shape[1] // 2
    s = jnp.concatenate(
        [cut(blocks[:experts], lefts[0], run), cut(blocks[experts:], lefts[1], run)], axis=1
    )
    sums = 0.0
    for at, size in steps(w_out.shape[0], 256):
        up = dot(w_out[at : at + size, :], s, NT)
        sums = sums + gate_sums(act[at : at + size, :], up)
        grad[at : at + size, :] = (up * slope[at : at + size, :].astype(f32)).astype(bf16)
    gates[...] = sums
    for at, size in steps(w_in.shape[1], 256):
        total[:, at : at + size] = dot(grad[...], w_in[:, at : at + size], TN)


def far_kernel(experts, block, capacity, pos, w_in, w_out, act, slope, near_total, near_gates, *refs):
    blocks, outs, (total, gates) = refs[: 2 * experts], refs[2 * experts : -2], refs[-2:]
    step, last = pl.program_id(0), pl.num_programs(0) - 1

    @pl.when(step == 0)
    def _():
        total[...] = near_total[...]
        gates[...] = near_gates[...]

    up = dot(w_out[...], stack(blocks, experts), NT)
    gates[...] += gate_sums(act[...], up)
    total[...] += dot((up * slope[...].astype(f32)).astype(bf16), w_in[...], TN)

    @pl.when(step == last)
    def _():
        rows = total[...].astype(bf16)
        gate_rows = gates[...].astype(bf16)
        for k, out in enumerate(outs):
            out[...] = rows[k * block : (k + 1) * block]
            out[capacity : capacity + 1, 0:block] = gate_rows[:, k * block : (k + 1) * block]


def cut(refs, left, size):
    return jnp.concatenate([ref[:, left : left + size] for ref in refs], axis=0)


def outer_rows(experts, own, other, refs):
    return dot(own[...], stack(refs[:experts], experts)) + dot(
        other[...], stack(refs[experts : 2 * experts], experts)
    )


def away_kernel(experts, owners, r, left, right, pos, own, other, *refs):
    out = refs[-1]
    size = own.shape[0] // owners
    mine = pl.ds(pl.multiple_of(lax.rem(pos[1] + r, owners) * size, size), size)
    for at, run in steps(out.shape[1], 256):
        total = dot(own[mine, :], cut(refs[:experts], left + at, run))
        total += dot(other[mine, :], cut(refs[experts : 2 * experts], right + at, run))
        out[:, at : at + run] = total.astype(out.dtype)


def home_kernel(experts, owners, pos, own, other, *refs):
    total = outer_rows(experts, own, other, refs)
    for ref in refs[2 * experts : 2 * experts + owners - 1]:
        total = total + ref[...].astype(f32)
    refs[-1][0] = total


def after_kernel(owners, before, *refs):
    total = before[...]
    for ref in refs[: owners - 1]:
        total = total + ref[...].astype(f32)
    refs[-1][0] = total


def gathered(meta, refs, experts, block):
    first, second = picks(meta[0:1, :], meta[1:2, :], experts * block)
    chosen = jnp.where(first | second, 1.0, 0.0).astype(bf16)
    return dot(chosen, stack(refs, experts), TN)


def gate_rows(meta, refs, block, capacity):
    values = jnp.concatenate([ref[capacity : capacity + 1, 0:block] for ref in refs], axis=0)
    out = []
    for at in (0, 1):
        flat = meta[at : at + 1, :].astype(jnp.int32)
        live = flat >= 0
        which = jnp.where(live, flat, 0) // block
        where = flat - which * block
        lane = lax.broadcasted_iota(jnp.int32, (block, flat.shape[1]), 0)
        hit = jnp.where((lane == where) & live, 1.0, 0.0).astype(bf16)
        by_block = dot(values, hit)
        mine = lax.broadcasted_iota(jnp.int32, by_block.shape, 0) == which
        gate = jnp.sum(jnp.where(mine, by_block, 0.0), axis=0, keepdims=True)
        out.append(jnp.where(live, gate / meta[at + 2 : at + 3, :], 0.0))
    return out


def collect_kernel(experts, block, capacity, meta, *refs):
    blocks, (grad_tokens, grad_combine) = refs[:experts], refs[experts:]
    grad_tokens[...] = gathered(meta, blocks, experts, block).astype(bf16)

    @pl.when(pl.program_id(0) == 0)
    def _():
        gates = gate_rows(meta, blocks, block, capacity)
        grad_combine[...] = jnp.concatenate(gates, axis=0).astype(bf16)


def shaped(shape, dtype=bf16):
    return jax.ShapeDtypeStruct(shape, dtype)


def full(array):
    return pl.BlockSpec(array.shape, lambda g, *pos, rank=array.ndim: (0,) * rank)


def columns(array, parts, first=0):
    size = array.shape[-1] // parts
    lead = array.shape[:-1]
    return pl.BlockSpec(
        lead + (size,), lambda g, *pos, rank=array.ndim: (0,) * (rank - 1) + (first + g,)
    )


def rows(array, size):
    return pl.BlockSpec((size, array.shape[1]), lambda g, *pos: (g, 0))


def share_rows(array, owners, r):
    return pl.BlockSpec(
        (array.shape[0] // owners, array.shape[1]), lambda g, pos: (lax.rem(pos[1] + r, owners), 0)
    )


def half_rows(array, parts, far=0):
    size = array.shape[1] // 2 // parts
    return pl.BlockSpec(
        (None, size, array.shape[2]), lambda g, pos: (0, (pos[0] ^ far) * parts + g, 0)
    )


def call(kernel, grid, scalars, operands, results, scratch=(), flops=0, alias=None):
    arrays, in_specs = [a for a, _ in operands], [s for _, s in operands]
    outs, out_specs = [a for a, _ in results], [s for _, s in results]
    moved = sum(a.size * a.dtype.itemsize for a in arrays + outs)
    return pl.pallas_call(
        kernel,
        out_shape=outs,
        grid_spec=pltpu.PrefetchScalarGridSpec(
            num_scalar_prefetch=len(scalars),
            grid=(grid,),
            in_specs=in_specs,
            out_specs=out_specs,
            scratch_shapes=list(scratch),
        ),
        input_output_aliases=alias or {},
        compiler_params=pltpu.CompilerParams(vmem_limit_bytes=28 << 20),
        cost_estimate=pl.CostEstimate(flops=int(flops), transcendentals=0, bytes_accessed=moved),
    )(*scalars, *arrays)


def direct(kernel, scalars, arrays, outs, flops=0):
    moved = sum(a.size * a.dtype.itemsize for a in list(arrays) + outs)
    return pl.pallas_call(
        kernel,
        out_shape=outs,
        in_specs=[pl.BlockSpec(memory_space=pltpu.SMEM)] * len(scalars)
        + [pl.BlockSpec(memory_space=pltpu.VMEM)] * len(arrays),
        out_specs=[pl.BlockSpec(memory_space=pltpu.VMEM)] * len(outs),
        compiler_params=pltpu.CompilerParams(vmem_limit_bytes=28 << 20),
        cost_estimate=pl.CostEstimate(flops=int(flops), transcendentals=0, bytes_accessed=moved),
    )(*scalars, *arrays)


def window(arrays, start, size):
    return [
        (a, pl.BlockSpec((a.shape[0], size), lambda g, *pos: (0, start // size))) for a in arrays
    ]


def runs_of(arrays, start, run):
    return [
        (a, pl.BlockSpec((a.shape[0], run), lambda g, *pos: (0, start // run + g))) for a in arrays
    ]


def per_device(tokens, grad_out, routes, keep_second, combine, w_in, w_out):
    experts, planes = lax.axis_size("expert"), lax.axis_size("dp")
    count, width = tokens.shape
    capacity = 5 * count // (2 * experts)
    block = -(-(capacity + 1) // 16) * 16
    owners = planes // 2
    units = w_in.shape[1] // 2
    share = units // owners
    slots = experts * block
    if planes % 2 or experts & (experts - 1):
        raise ValueError("mesh sizes")
    plane = lax.axis_index("dp")
    pos = jnp.stack([plane // owners, plane % owners]).astype(jnp.int32)
    bind = functools.partial

    def across(value):
        return lax.ppermute(value, "dp", [(j, (j + owners) % planes) for j in range(planes)])

    def exchange(values):
        return [values[0]] + [
            lax.ppermute(values[k], "expert", [(i, i ^ k) for i in range(experts)])
            for k in range(1, experts)
        ]

    def to_owners(values):
        return [
            lax.ppermute(
                value,
                "dp",
                [(j, j // owners * owners + (j + r + 1) % owners) for j in range(planes)],
            )
            for r, value in enumerate(values)
        ]

    def each(arrays, spec, *more):
        return [(a, spec(a, *more)) for a in arrays]

    routes_t, keep_t, combine_t = routes.T, keep_second.reshape(1, count), combine.T

    def stay(array):
        return pltpu.with_memory_space_constraint(array, pltpu.HBM)

    other_x = across(tokens)
    half = width // 2
    other_dya = across(grad_out[:, :half])
    other_dyb = across(grad_out[:, half:])

    def blocks(columns_of):
        return [shaped((block, columns_of))] * experts

    act_shape = shaped((units, slots))
    unit_parts = max(units // 256, 1)
    unit_rows = units // unit_parts
    meta_shape = shaped((8, count), f32)
    meta, *own_xs = call(
        bind(own_send_kernel, experts, block, capacity),
        1,
        [],
        each([stay(a) for a in (routes_t, keep_t, combine_t, tokens)], full)
        + window([stay(grad_out)], 0, half),
        each([meta_shape] + blocks(width + half), full),
        flops=3 * slots * count * width,
    )
    own_xs = exchange(own_xs)
    half_in, half_out = call(
        load_kernel,
        4,
        [pos],
        each([stay(w_in), stay(w_out)], half_rows, 4),
        each([shaped((units, width))] * 2, rows, units // 4),
    )
    other_meta = across(meta)
    other_xb = call(
        bind(send_x_kernel, experts, block),
        2,
        [],
        each([other_meta], full) + each([other_x], columns, 2),
        each(blocks(width), columns, 2),
        flops=2 * slots * count * width,
    )
    x_out = exchange(other_xb)
    sb_out = call(
        bind(send_s_kernel, experts, block),
        1,
        [],
        each([meta], full) + window([stay(grad_out)], half, half),
        window(blocks(2 * half), 0, half),
        flops=slots * count * width,
    )
    sa_out = call(
        bind(send_s_kernel, experts, block),
        1,
        [],
        each([other_meta, other_dya], full),
        each(blocks(half), full),
        flops=slots * count * width,
    )
    sa_out = exchange(sa_out)
    sb_out = call(
        bind(send_s_kernel, experts, block),
        1,
        [],
        each([other_meta, other_dyb], full)
        + [(a, pl.BlockSpec(memory_space=pl.ANY)) for a in sb_out],
        window(blocks(2 * half), half, half),
        flops=slots * count * width,
        alias={2 + k: k for k in range(experts)},
    )
    sb_out = exchange(sb_out)
    own_x, other_x = (own_xs, 0), (x_out, 0)
    own_sa, other_sa = (own_xs, width), (sa_out, 0)
    own_sb, other_sb = (sb_out, 0), (sb_out, half)

    def act(x):
        return direct(
            bind(act_kernel, x[1]), [], [half_in] + x[0], [act_shape] * 2, 2 * slots * units * width
        )

    own_act, own_slope = act(own_x)
    other_act, other_slope = act(other_x)
    far_act, far_slope = call(
        bind(far_act_kernel, experts),
        unit_parts,
        [pos],
        each([stay(w_in)], half_rows, unit_parts, 1) + window(*own_x, width),
        each([act_shape] * 2, rows, unit_rows),
        flops=2 * slots * units * width,
    )
    run = width // 4
    fed = slots * share * run

    def away(acts, left, right, first, many):
        return [
            direct(
                bind(
                    away_kernel, experts, owners, r, left[1] + first * run, right[1] + first * run
                ),
                [pos],
                acts + left[0] + right[0],
                [shaped((share, many * run))],
                4 * fed * many,
            )[0]
            for r in range(1, owners)
        ]

    goal = shaped((1, share, width), f32)

    def into(array, operands, prefetched):
        if array is None:
            return operands, None
        return operands + [(array, pl.BlockSpec(memory_space=pl.ANY))], {
            len(operands) + prefetched: 0
        }

    def home(acts, left, right, got, first, many, array=None):
        operands, alias = into(
            array,
            each(acts, share_rows, owners, 0)
            + runs_of(*left, run)
            + runs_of(*right, run)
            + each(got, columns, many),
            1,
        )
        return call(
            bind(home_kernel, experts, owners),
            many,
            [pos],
            operands,
            each([goal], columns, 4, first),
            flops=4 * fed * many,
            alias=alias,
        )[0]

    def after(before, got, first, many, array=None):
        operands, alias = into(
            array, runs_of([before], first * run, run) + each(got, columns, many), 0
        )
        return call(
            bind(after_kernel, owners),
            many,
            [],
            operands,
            each([goal], columns, 4, first),
            alias=alias,
        )[0]

    out_acts = [own_act, other_act]
    away_oa = away(out_acts, own_sa, other_sa, 0, 2)
    got_oa = to_owners(away_oa)
    away_ob = away(out_acts, own_sb, other_sb, 0, 2)
    got_ob = to_owners(away_ob)
    total_shape, gate_shape = shaped((slots, width), f32), shaped((1, slots), f32)
    own_grad, near_total, near_gates = direct(
        bind(own_grad_kernel, experts, (own_sa[1], own_sb[1])),
        [],
        [half_in, half_out, own_act, own_slope] + own_sa[0] + own_sb[0],
        [act_shape, total_shape, gate_shape],
        4 * slots * units * width,
    )
    other_grad = direct(
        bind(other_grad_kernel, experts, (other_sa[1], other_sb[1])),
        [],
        [half_out, other_slope] + other_sa[0] + other_sb[0],
        [act_shape],
        2 * slots * units * width,
    )[0]
    own_back = call(
        bind(far_kernel, experts, block, capacity),
        unit_parts,
        [pos],
        each([stay(w_in), stay(w_out)], half_rows, unit_parts, 1)
        + each([far_act, far_slope], rows, unit_rows)
        + each([near_total, near_gates], full)
        + window(*own_sa, half)
        + window(*own_sb, half),
        each(blocks(width), full),
        [pltpu.VMEM((slots, width), f32), pltpu.VMEM((1, slots), f32)],
        4 * slots * units * width,
    )
    in_acts = [own_grad, other_grad]
    away_a = away(in_acts, own_x, other_x, 0, 3)
    got_a = to_owners(away_a)
    away_b = away(in_acts, own_x, other_x, 3, 1)
    got_b = to_owners(away_b)
    own_back = exchange(own_back)

    grad_outw = home(out_acts, own_sa, other_sa, got_oa, 0, 2)
    grad_outw = home(out_acts, own_sb, other_sb, got_ob, 2, 2, grad_outw)
    grad_tokens, grad_combine = call(
        bind(collect_kernel, experts, block, capacity),
        2,
        [],
        each([meta], full) + each(own_back, columns, 2),
        each([shaped((count, width))], columns, 2) + each([shaped((2, count))], full),
        flops=2 * slots * count * width,
    )
    before = direct(
        bind(away_kernel, experts, owners, 0, own_x[1], other_x[1]),
        [pos],
        in_acts + own_x[0] + other_x[0],
        [shaped((share, width), f32)],
        16 * fed,
    )[0]
    grad_in = after(before, got_a, 0, 3)
    grad_in = after(before, got_b, 3, 1, grad_in)
    return grad_tokens, grad_combine.T, grad_in, grad_outw


def solution(mesh):
    return jax.shard_map(
        per_device,
        mesh=mesh,
        in_specs=(
            P(("expert", "dp"), None),
            P(("expert", "dp"), None),
            P(("expert", "dp"), None),
            P(("expert", "dp")),
            P(("expert", "dp"), None),
            P("expert", None, None),
            P("expert", None, None),
        ),
        out_specs=(
            P(("expert", "dp"), None),
            P(("expert", "dp"), None),
            P("expert", "dp", None),
            P("expert", "dp", None),
        ),
        check_vma=False,
    )
```

```python
import functools

import jax
import jax.numpy as jnp
from jax import lax
from jax.experimental import pallas as pl
from jax.experimental.pallas import tpu as pltpu
from jax.sharding import PartitionSpec as P


root_coef = 0.7978845608
cube_coef = 0.044715
bf16 = jnp.bfloat16
f32 = jnp.float32

NN = (((1,), (0,)), ((), ()))
NT = (((1,), (1,)), ((), ()))
TN = (((0,), (0,)), ((), ()))


def dot(a, b, dims=NN):
    return lax.dot_general(a, b, dims, preferred_element_type=f32)


def gelu_slope(hidden):
    square = hidden * hidden
    tanh_val = jnp.tanh(hidden * (root_coef + (root_coef * cube_coef) * square))
    half_up = 0.5 + 0.5 * tanh_val
    active = hidden * half_up
    derivative = half_up + active * (1.0 - half_up) * (
        2.0 * root_coef + (6.0 * root_coef * cube_coef) * square
    )
    return active, derivative


def steps(extent, most):
    return [(at, min(most, extent - at)) for at in range(0, extent, most)]


def stack(refs, experts):
    runs = [
        jnp.concatenate([ref[...] for ref in refs[at : at + experts]], axis=0)
        for at in range(0, len(refs), experts)
    ]
    return runs[0] if len(runs) == 1 else jnp.concatenate(runs, axis=1)


def slot_rows(routes, keep, combine, me, experts, block, capacity):
    count = routes.shape[1]
    kept = keep > 0
    first, second = routes[0:1, :] ^ me, routes[1:2, :] ^ me
    ids = lax.broadcasted_iota(jnp.int32, (experts, count), 0)
    first_hot = jnp.where(first == ids, 1.0, 0.0)
    second_hot = jnp.where((second == ids) & kept, 1.0, 0.0)
    earlier = jnp.where(
        lax.broadcasted_iota(jnp.int32, (count, count), 0)
        < lax.broadcasted_iota(jnp.int32, (count, count), 1),
        1.0,
        0.0,
    ).astype(bf16)
    first_pos = dot(first_hot.astype(bf16), earlier)
    second_pos = dot(second_hot.astype(bf16), earlier) + jnp.sum(first_hot, axis=1, keepdims=True)
    first_slot = jnp.sum(first_pos * first_hot, axis=0, keepdims=True)
    second_slot = jnp.sum(second_pos * second_hot, axis=0, keepdims=True)
    first_flat = jnp.where(first_slot < capacity, first.astype(f32) * block + first_slot, -1.0)
    second_flat = jnp.where(
        kept & (second_slot < capacity), second.astype(f32) * block + second_slot, -1.0
    )
    weights = combine.astype(f32)
    return first_flat, second_flat, weights[0:1, :], weights[1:2, :]


def picks(first_flat, second_flat, rows):
    ids = lax.broadcasted_iota(jnp.int32, (rows, first_flat.shape[1]), 0)
    return ids == first_flat.astype(jnp.int32), ids == second_flat.astype(jnp.int32)


def place(pick, source, out_refs, block, left=0, begin=0, end=None):
    end = source.shape[1] if end is None else end
    for at, size in steps(end - begin, 256):
        rows = dot(pick, source[:, begin + at : begin + at + size]).astype(bf16)
        for k, out in enumerate(out_refs):
            out[:, left + at : left + at + size] = rows[k * block : (k + 1) * block]


def own_send_kernel(
    experts, block, capacity, routes, keep, combine, tokens, grad_out, meta, lefts, rights, *outs
):
    end = lefts.shape[1]
    lefts[...] = grad_out[:, :end]
    rights[...] = grad_out[:, end:]
    me = lax.axis_index("expert")
    a, b, c, d = slot_rows(routes[...], keep[...], combine[...], me, experts, block, capacity)
    meta[0:1, :] = a
    meta[1:2, :] = b
    meta[2:3, :] = c
    meta[3:4, :] = d
    meta[4:8, :] = jnp.zeros((4, a.shape[1]), f32)
    first, second = picks(a, b, experts * block)
    place(jnp.where(first | second, 1.0, 0.0).astype(bf16), tokens, outs, block)
    weighted = jnp.where(first, c, jnp.where(second, d, 0.0)).astype(bf16)
    place(weighted, grad_out, outs, block, tokens.shape[1], 0, end)


def load_kernel(pos, w_in, w_out, in_half, out_half):
    in_half[...] = w_in[...]
    out_half[...] = w_out[...]


def send_x_kernel(experts, block, meta, tokens, *outs):
    first, second = picks(meta[0:1, :], meta[1:2, :], experts * block)
    place(jnp.where(first | second, 1.0, 0.0).astype(bf16), tokens, outs, block)


def send_s_kernel(experts, block, begin, meta, grad_out, *refs):
    first, second = picks(meta[0:1, :], meta[1:2, :], experts * block)
    weighted = jnp.where(first, meta[2:3, :], jnp.where(second, meta[3:4, :], 0.0))
    place(weighted.astype(bf16), grad_out, refs[-experts:], block, 0, begin)


def gate_sums(active, up):
    return jnp.sum(active.astype(f32) * up, axis=0, keepdims=True)


def act_rows(weights, x, act, slope, at, size):
    active, derivative = gelu_slope(dot(weights, x, NT))
    act[at : at + size, :] = active.astype(bf16)
    slope[at : at + size, :] = derivative.astype(bf16)


def act_kernel(left, w_in, *refs):
    blocks, (act, slope) = refs[:-2], refs[-2:]
    x = cut(blocks, left, w_in.shape[1])
    for at, size in steps(w_in.shape[0], 256):
        act_rows(w_in[at : at + size, :], x, act, slope, at, size)


def far_act_kernel(experts, pos, w_in, *refs):
    act_rows(w_in[...], stack(refs[:-2], experts), *refs[-2:], 0, w_in.shape[0])


def other_grad_kernel(experts, sa, sb, w_out, slope, *refs):
    s = jnp.concatenate([cut(refs[:experts], *sa), cut(refs[experts : 2 * experts], *sb)], axis=1)
    for at, size in steps(w_out.shape[0], 256):
        up = dot(w_out[at : at + size, :], s, NT)
        refs[-1][at : at + size, :] = (up * slope[at : at + size, :].astype(f32)).astype(bf16)


def own_grad_kernel(experts, sa, sb, w_in, w_out, act, slope, *refs):
    blocks, (grad, total, gates, scaled) = refs[:-4], refs[-4:]
    s = jnp.concatenate([cut(blocks[:experts], *sa), cut(blocks[experts:], *sb)], axis=1)
    scaled[...] = s
    sums = 0.0
    for at, size in steps(w_out.shape[0], 256):
        up = dot(w_out[at : at + size, :], s, NT)
        sums = sums + gate_sums(act[at : at + size, :], up)
        grad[at : at + size, :] = (up * slope[at : at + size, :].astype(f32)).astype(bf16)
    gates[...] = sums
    for at, size in steps(w_in.shape[1], 256):
        total[:, at : at + size] = dot(grad[...], w_in[:, at : at + size], TN)


def far_kernel(block, capacity, pos, w_in, w_out, act, slope, near_total, near_gates, scaled, *refs):
    outs, (total, gates) = refs[:-2], refs[-2:]
    step, last = pl.program_id(0), pl.num_programs(0) - 1

    @pl.when(step == 0)
    def _():
        total[...] = near_total[...]
        gates[...] = near_gates[...]

    up = dot(w_out[...], scaled[...], NT)
    gates[...] += gate_sums(act[...], up)
    total[...] += dot((up * slope[...].astype(f32)).astype(bf16), w_in[...], TN)

    @pl.when(step == last)
    def _():
        rows = total[...].astype(bf16)
        gate_rows = gates[...].astype(bf16)
        for k, out in enumerate(outs):
            out[...] = rows[k * block : (k + 1) * block]
            out[capacity : capacity + 1, 0:block] = gate_rows[:, k * block : (k + 1) * block]


def cut(refs, left, size):
    return jnp.concatenate([ref[:, left : left + size] for ref in refs], axis=0)


def away_kernel(experts, owners, r, left, right, pos, own, other, *refs):
    out = refs[-1]
    size = own.shape[0] // owners
    mine = pl.ds(pl.multiple_of(lax.rem(pos[1] + r, owners) * size, size), size)
    for at, run in steps(out.shape[1], 256):
        total = dot(own[mine, :], cut(refs[:experts], left + at, run))
        total += dot(other[mine, :], cut(refs[experts : 2 * experts], right + at, run))
        out[:, at : at + run] = total.astype(out.dtype)


def home_kernel(experts, owners, parts, pos, own, other, *refs):
    out, total, sems = refs[-3:]
    size = own.shape[0] // owners
    mine = pl.ds(pl.multiple_of(pos[1] * size, size), size)
    per, column, copies = 2 * experts + owners - 1, 0, []
    for number, (left, right, extent) in enumerate(parts):
        blocks = refs[number * per : (number + 1) * per]
        for at, run in steps(extent, 256):
            rows = dot(own[mine, :], cut(blocks[:experts], left + at, run))
            rows += dot(other[mine, :], cut(blocks[experts : 2 * experts], right + at, run))
            for ref in blocks[2 * experts :]:
                rows += ref[:, at : at + run].astype(f32)
            total[:, column : column + run] = rows
            here = slice(column, column + run)
            copy = pltpu.make_async_copy(
                total.at[:, here], out.at[0, :, here], sems.at[len(copies)]
            )
            copy.start()
            copies.append(copy)
            column += run
    for copy in copies:
        copy.wait()


def after_kernel(owners, before, *refs):
    total = before[...]
    for ref in refs[: owners - 1]:
        total = total + ref[...].astype(f32)
    refs[-1][0] = total


def gathered(meta, refs, experts, block):
    first, second = picks(meta[0:1, :], meta[1:2, :], experts * block)
    chosen = jnp.where(first | second, 1.0, 0.0).astype(bf16)
    return dot(chosen, stack(refs, experts), TN)


def gate_rows(meta, refs, block, capacity):
    values = jnp.concatenate([ref[capacity : capacity + 1, 0:block] for ref in refs], axis=0)
    out = []
    for at in (0, 1):
        flat = meta[at : at + 1, :].astype(jnp.int32)
        live = flat >= 0
        which = jnp.where(live, flat, 0) // block
        where = flat - which * block
        lane = lax.broadcasted_iota(jnp.int32, (block, flat.shape[1]), 0)
        hit = jnp.where((lane == where) & live, 1.0, 0.0).astype(bf16)
        by_block = dot(values, hit)
        mine = lax.broadcasted_iota(jnp.int32, by_block.shape, 0) == which
        gate = jnp.sum(jnp.where(mine, by_block, 0.0), axis=0, keepdims=True)
        out.append(jnp.where(live, gate / meta[at + 2 : at + 3, :], 0.0))
    return out


def collect_kernel(experts, block, capacity, meta, *refs):
    blocks, (grad_tokens, grad_combine) = refs[:experts], refs[experts:]
    grad_tokens[...] = gathered(meta, blocks, experts, block).astype(bf16)

    @pl.when(pl.program_id(0) == 0)
    def _():
        gates = gate_rows(meta, blocks, block, capacity)
        grad_combine[...] = jnp.concatenate(gates, axis=0).astype(bf16)


def shaped(shape, dtype=bf16):
    return jax.ShapeDtypeStruct(shape, dtype)


def full(array):
    return pl.BlockSpec(array.shape, lambda g, *pos, rank=array.ndim: (0,) * rank)


def columns(array, parts, first=0):
    size = array.shape[-1] // parts
    lead = array.shape[:-1]
    return pl.BlockSpec(
        lead + (size,), lambda g, *pos, rank=array.ndim: (0,) * (rank - 1) + (first + g,)
    )


def rows(array, size):
    return pl.BlockSpec((size, array.shape[1]), lambda g, *pos: (g, 0))


def half_rows(array, parts, far=0):
    size = array.shape[1] // 2 // parts
    return pl.BlockSpec(
        (None, size, array.shape[2]), lambda g, pos: (0, (pos[0] ^ far) * parts + g, 0)
    )


def call(kernel, grid, scalars, operands, results, scratch=(), flops=0, alias=None):
    arrays, in_specs = [a for a, _ in operands], [s for _, s in operands]
    outs, out_specs = [a for a, _ in results], [s for _, s in results]
    moved = sum(a.size * a.dtype.itemsize for a in arrays + outs)
    return pl.pallas_call(
        kernel,
        out_shape=outs,
        grid_spec=pltpu.PrefetchScalarGridSpec(
            num_scalar_prefetch=len(scalars),
            grid=(grid,),
            in_specs=in_specs,
            out_specs=out_specs,
            scratch_shapes=list(scratch),
        ),
        input_output_aliases=alias or {},
        compiler_params=pltpu.CompilerParams(vmem_limit_bytes=28 << 20),
        cost_estimate=pl.CostEstimate(flops=int(flops), transcendentals=0, bytes_accessed=moved),
    )(*scalars, *arrays)


def direct(kernel, scalars, arrays, outs, flops=0):
    moved = sum(a.size * a.dtype.itemsize for a in list(arrays) + outs)
    return pl.pallas_call(
        kernel,
        out_shape=outs,
        in_specs=[pl.BlockSpec(memory_space=pltpu.SMEM)] * len(scalars)
        + [pl.BlockSpec(memory_space=pltpu.VMEM)] * len(arrays),
        out_specs=[pl.BlockSpec(memory_space=pltpu.VMEM)] * len(outs),
        compiler_params=pltpu.CompilerParams(vmem_limit_bytes=28 << 20),
        cost_estimate=pl.CostEstimate(flops=int(flops), transcendentals=0, bytes_accessed=moved),
    )(*scalars, *arrays)


def window(arrays, start, size):
    return [
        (a, pl.BlockSpec((a.shape[0], size), lambda g, *pos: (0, start // size))) for a in arrays
    ]


def runs_of(arrays, start, run):
    return [
        (a, pl.BlockSpec((a.shape[0], run), lambda g, *pos: (0, start // run + g))) for a in arrays
    ]


def per_device(tokens, grad_out, routes, keep_second, combine, w_in, w_out):
    experts, planes = lax.axis_size("expert"), lax.axis_size("dp")
    count, width = tokens.shape
    capacity = 5 * count // (2 * experts)
    block = -(-(capacity + 1) // 16) * 16
    owners = planes // 2
    units = w_in.shape[1] // 2
    share = units // owners
    slots = experts * block
    if planes % 2 or experts & (experts - 1):
        raise ValueError("mesh sizes")
    plane = lax.axis_index("dp")
    pos = jnp.stack([plane // owners, plane % owners]).astype(jnp.int32)
    bind = functools.partial

    def across(value):
        return lax.ppermute(value, "dp", [(j, (j + owners) % planes) for j in range(planes)])

    def exchange(values, which=None):
        sent = [
            lax.ppermute(values[k], "expert", [(i, i ^ k) for i in range(experts)])
            for k in which or range(1, experts)
        ]
        return sent if which else [values[0]] + sent

    def to_owners(values):
        return [
            lax.ppermute(
                value,
                "dp",
                [(j, j // owners * owners + (j + r + 1) % owners) for j in range(planes)],
            )
            for r, value in enumerate(values)
        ]

    def each(arrays, spec, *more):
        return [(a, spec(a, *more)) for a in arrays]

    routes_t, keep_t, combine_t = routes.T, keep_second.reshape(1, count), combine.T

    def stay(array):
        return pltpu.with_memory_space_constraint(array, pltpu.HBM)

    other_x = across(tokens)
    half = width // 2
    rest = width - half
    half = width // 2
    rest = width - half

    def blocks(columns_of):
        return [shaped((block, columns_of))] * experts

    act_shape = shaped((units, slots))
    unit_parts = max(units // 256, 1)
    unit_rows = units // unit_parts
    meta_shape = shaped((8, count), f32)
    meta, dya, dyb, *own_xs = call(
        bind(own_send_kernel, experts, block, capacity),
        1,
        [],
        each([stay(a) for a in (routes_t, keep_t, combine_t, tokens, grad_out)], full),
        each(
            [meta_shape, shaped((count, half)), shaped((count, rest))] + blocks(width + half),
            full,
        ),
        flops=3 * slots * count * width,
    )
    own_xs = exchange(own_xs)
    half_in, half_out = call(
        load_kernel,
        4,
        [pos],
        each([stay(w_in), stay(w_out)], half_rows, 4),
        each([shaped((units, width))] * 2, rows, units // 4),
    )
    other_dya = across(dya)
    other_dyb = across(dyb)
    other_meta = across(meta)
    other_xb = call(
        bind(send_x_kernel, experts, block),
        2,
        [],
        each([other_meta], full) + each([other_x], columns, 2),
        each(blocks(width), columns, 2),
        flops=2 * slots * count * width,
    )
    x_out = exchange(other_xb)
    sb_out = call(
        bind(send_s_kernel, experts, block, 0),
        1,
        [],
        each([meta, dyb], full),
        window(blocks(2 * rest), 0, rest),
        flops=slots * count * width,
    )
    sa_out = call(
        bind(send_s_kernel, experts, block, 0),
        1,
        [],
        each([other_meta, other_dya], full),
        each(blocks(half), full),
        flops=slots * count * width,
    )
    sa_out = exchange(sa_out)
    sb_out = call(
        bind(send_s_kernel, experts, block, 0),
        1,
        [],
        each([other_meta, other_dyb], full)
        + [(a, pl.BlockSpec(memory_space=pl.ANY)) for a in sb_out],
        window(blocks(2 * rest), rest, rest),
        flops=slots * count * width,
        alias={2 + k: k for k in range(experts)},
    )
    near = experts * 3 // 4
    sb_far = exchange(sb_out, range(near, experts))
    sb_out = [sb_out[0]] + exchange(sb_out, range(1, near)) + sb_far
    own_x, other_x = (own_xs, 0), (x_out, 0)
    own_sa, other_sa = (own_xs, width), (sa_out, 0)
    own_sb, other_sb = (sb_out, 0), (sb_out, rest)

    def act(x):
        return direct(
            bind(act_kernel, x[1]), [], [half_in] + x[0], [act_shape] * 2, 2 * slots * units * width
        )

    own_act, own_slope = act(own_x)
    other_act, other_slope = act(other_x)
    far_act, far_slope = call(
        bind(far_act_kernel, experts),
        unit_parts,
        [pos],
        each([stay(w_in)], half_rows, unit_parts, 1) + window(*own_x, width),
        each([act_shape] * 2, rows, unit_rows),
        flops=2 * slots * units * width,
    )
    run = width // 4
    fed = slots * share * run

    def away(acts, left, right, first, extent):
        return [
            direct(
                bind(away_kernel, experts, owners, r, left[1] + first, right[1] + first),
                [pos],
                acts + left[0] + right[0],
                [shaped((share, extent))],
                4 * slots * share * extent,
            )[0]
            for r in range(1, owners)
        ]

    goal = shaped((1, share, width), f32)

    def into(array, operands, prefetched):
        if array is None:
            return operands, None
        return operands + [(array, pl.BlockSpec(memory_space=pl.ANY))], {
            len(operands) + prefetched: 0
        }

    def after(before, got, first, many, array=None):
        operands, alias = into(
            array, runs_of([before], first * run, run) + each(got, columns, many), 0
        )
        return call(
            bind(after_kernel, owners),
            many,
            [],
            operands,
            each([goal], columns, 4, first),
            alias=alias,
        )[0]

    out_acts = [own_act, other_act]
    away_oa = away(out_acts, own_sa, other_sa, 0, half)
    got_oa = to_owners(away_oa)
    away_ob = away(out_acts, own_sb, other_sb, 0, rest)
    got_ob = to_owners(away_ob)
    total_shape, gate_shape = shaped((slots, width), f32), shaped((1, slots), f32)
    own_grad, near_total, near_gates, own_scaled = direct(
        bind(own_grad_kernel, experts, (own_sa[1], half), (own_sb[1], rest)),
        [],
        [half_in, half_out, own_act, own_slope] + own_sa[0] + own_sb[0],
        [act_shape, total_shape, gate_shape, shaped((slots, width))],
        4 * slots * units * width,
    )
    other_grad = direct(
        bind(other_grad_kernel, experts, (other_sa[1], half), (other_sb[1], rest)),
        [],
        [half_out, other_slope] + other_sa[0] + other_sb[0],
        [act_shape],
        2 * slots * units * width,
    )[0]
    own_back = call(
        bind(far_kernel, block, capacity),
        unit_parts,
        [pos],
        each([stay(w_in), stay(w_out)], half_rows, unit_parts, 1)
        + each([far_act, far_slope], rows, unit_rows)
        + each([near_total, near_gates, own_scaled], full),
        each(blocks(width), full),
        [pltpu.VMEM((slots, width), f32), pltpu.VMEM((1, slots), f32)],
        4 * slots * units * width,
    )
    in_acts = [own_grad, other_grad]
    away_a = away(in_acts, own_x, other_x, 0, 3 * run)
    got_a = to_owners(away_a)
    away_b = away(in_acts, own_x, other_x, 3 * run, run)
    got_b = to_owners(away_b)
    own_back = exchange(own_back)

    operands = (
        out_acts
        + own_sa[0]
        + other_sa[0]
        + got_oa
        + own_sb[0]
        + other_sb[0]
        + got_ob
    )
    parts = ((own_sa[1], other_sa[1], half), (own_sb[1], other_sb[1], rest))
    grad_outw = pl.pallas_call(
        bind(home_kernel, experts, owners, parts),
        name="home_out",
        out_shape=goal,
        in_specs=[pl.BlockSpec(memory_space=pltpu.SMEM)]
        + [pl.BlockSpec(memory_space=pltpu.VMEM)] * len(operands),
        out_specs=pl.BlockSpec(memory_space=pl.ANY),
        scratch_shapes=[
            pltpu.VMEM((share, width), f32),
            pltpu.SemaphoreType.DMA((len(steps(half, 256)) + len(steps(rest, 256)),)),
        ],
        compiler_params=pltpu.CompilerParams(vmem_limit_bytes=28 << 20),
        cost_estimate=pl.CostEstimate(
            flops=4 * slots * share * width, transcendentals=0, bytes_accessed=12 * share * width
        ),
    )(pos, *operands)
    grad_tokens, grad_combine = call(
        bind(collect_kernel, experts, block, capacity),
        2,
        [],
        each([meta], full) + each(own_back, columns, 2),
        each([shaped((count, width))], columns, 2) + each([shaped((2, count))], full),
        flops=2 * slots * count * width,
    )
    before = direct(
        bind(away_kernel, experts, owners, 0, own_x[1], other_x[1]),
        [pos],
        in_acts + own_x[0] + other_x[0],
        [shaped((share, width), f32)],
        16 * fed,
    )[0]
    grad_in = after(before, got_a, 0, 3)
    grad_in = after(before, got_b, 3, 1, grad_in)
    return grad_tokens, grad_combine.T, grad_in, grad_outw


def solution(mesh):
    return jax.shard_map(
        per_device,
        mesh=mesh,
        in_specs=(
            P(("expert", "dp"), None),
            P(("expert", "dp"), None),
            P(("expert", "dp"), None),
            P(("expert", "dp")),
            P(("expert", "dp"), None),
            P("expert", None, None),
            P("expert", None, None),
        ),
        out_specs=(
            P(("expert", "dp"), None),
            P(("expert", "dp"), None),
            P("expert", "dp", None),
            P("expert", "dp", None),
        ),
        check_vma=False,
    )
```

```python
import functools

import jax
import jax.numpy as jnp
from jax import lax
from jax.experimental import pallas as pl
from jax.experimental.pallas import tpu as pltpu
from jax.sharding import PartitionSpec as P


root_coef = 0.7978845608
cube_coef = 0.044715
bf16 = jnp.bfloat16
f32 = jnp.float32

NN = (((1,), (0,)), ((), ()))
NT = (((1,), (1,)), ((), ()))
TN = (((0,), (0,)), ((), ()))


def dot(a, b, dims=NN):
    return lax.dot_general(a, b, dims, preferred_element_type=f32)


def gelu_slope(hidden):
    square = hidden * hidden
    tanh_val = jnp.tanh(hidden * (root_coef + (root_coef * cube_coef) * square))
    half_up = 0.5 + 0.5 * tanh_val
    active = hidden * half_up
    derivative = half_up + active * (1.0 - half_up) * (
        2.0 * root_coef + (6.0 * root_coef * cube_coef) * square
    )
    return active, derivative


def steps(extent, most):
    return [(at, min(most, extent - at)) for at in range(0, extent, most)]


def stack(refs, experts):
    runs = [
        jnp.concatenate([ref[...] for ref in refs[at : at + experts]], axis=0)
        for at in range(0, len(refs), experts)
    ]
    return runs[0] if len(runs) == 1 else jnp.concatenate(runs, axis=1)


def slot_rows(routes, keep, combine, me, experts, block, capacity):
    count = routes.shape[1]
    kept = keep > 0
    first, second = routes[0:1, :] ^ me, routes[1:2, :] ^ me
    ids = lax.broadcasted_iota(jnp.int32, (experts, count), 0)
    first_hot = jnp.where(first == ids, 1.0, 0.0)
    second_hot = jnp.where((second == ids) & kept, 1.0, 0.0)
    earlier = jnp.where(
        lax.broadcasted_iota(jnp.int32, (count, count), 0)
        < lax.broadcasted_iota(jnp.int32, (count, count), 1),
        1.0,
        0.0,
    ).astype(bf16)
    first_pos = dot(first_hot.astype(bf16), earlier)
    second_pos = dot(second_hot.astype(bf16), earlier) + jnp.sum(first_hot, axis=1, keepdims=True)
    first_slot = jnp.sum(first_pos * first_hot, axis=0, keepdims=True)
    second_slot = jnp.sum(second_pos * second_hot, axis=0, keepdims=True)
    first_flat = jnp.where(first_slot < capacity, first.astype(f32) * block + first_slot, -1.0)
    second_flat = jnp.where(
        kept & (second_slot < capacity), second.astype(f32) * block + second_slot, -1.0
    )
    weights = combine.astype(f32)
    return first_flat, second_flat, weights[0:1, :], weights[1:2, :]


def picks(first_flat, second_flat, rows):
    ids = lax.broadcasted_iota(jnp.int32, (rows, first_flat.shape[1]), 0)
    return ids == first_flat.astype(jnp.int32), ids == second_flat.astype(jnp.int32)


def place(pick, source, out_refs, block, left=0, begin=0, end=None):
    end = source.shape[1] if end is None else end
    for at, size in steps(end - begin, 256):
        rows = dot(pick, source[:, begin + at : begin + at + size]).astype(bf16)
        for k, out in enumerate(out_refs):
            out[:, left + at : left + at + size] = rows[k * block : (k + 1) * block]


def own_send_kernel(
    experts, block, capacity, routes, keep, combine, tokens, grad_out, meta, lefts, rights, *outs
):
    end = lefts.shape[1]
    lefts[...] = grad_out[:, :end]
    rights[...] = grad_out[:, end:]
    me = lax.axis_index("expert")
    a, b, c, d = slot_rows(routes[...], keep[...], combine[...], me, experts, block, capacity)
    meta[0:1, :] = a
    meta[1:2, :] = b
    meta[2:3, :] = c
    meta[3:4, :] = d
    meta[4:8, :] = jnp.zeros((4, a.shape[1]), f32)
    first, second = picks(a, b, experts * block)
    place(jnp.where(first | second, 1.0, 0.0).astype(bf16), tokens, outs, block)
    weighted = jnp.where(first, c, jnp.where(second, d, 0.0)).astype(bf16)
    place(weighted, grad_out, outs, block, tokens.shape[1], 0, end)


def load_kernel(pos, w_in, w_out, in_half, out_half):
    in_half[...] = w_in[...]
    out_half[...] = w_out[...]


def send_x_kernel(experts, block, meta, tokens, *outs):
    first, second = picks(meta[0:1, :], meta[1:2, :], experts * block)
    place(jnp.where(first | second, 1.0, 0.0).astype(bf16), tokens, outs, block)


def send_s_kernel(experts, block, begin, meta, grad_out, *refs):
    first, second = picks(meta[0:1, :], meta[1:2, :], experts * block)
    weighted = jnp.where(first, meta[2:3, :], jnp.where(second, meta[3:4, :], 0.0))
    place(weighted.astype(bf16), grad_out, refs[-experts:], block, 0, begin)


def gate_sums(active, up):
    return jnp.sum(active.astype(f32) * up, axis=0, keepdims=True)


def act_rows(weights, x, act, slope, at, size):
    active, derivative = gelu_slope(dot(weights, x, NT))
    act[at : at + size, :] = active.astype(bf16)
    slope[at : at + size, :] = derivative.astype(bf16)


def act_kernel(left, w_in, *refs):
    blocks, (act, slope) = refs[:-2], refs[-2:]
    x = cut(blocks, left, w_in.shape[1])
    for at, size in steps(w_in.shape[0], 256):
        act_rows(w_in[at : at + size, :], x, act, slope, at, size)


def far_act_kernel(experts, pos, w_in, *refs):
    act_rows(w_in[...], stack(refs[:-2], experts), *refs[-2:], 0, w_in.shape[0])


def other_grad_kernel(experts, sa, sb, w_out, slope, *refs):
    s = jnp.concatenate([cut(refs[:experts], *sa), cut(refs[experts : 2 * experts], *sb)], axis=1)
    for at, size in steps(w_out.shape[0], 256):
        up = dot(w_out[at : at + size, :], s, NT)
        refs[-1][at : at + size, :] = (up * slope[at : at + size, :].astype(f32)).astype(bf16)


def own_grad_kernel(experts, sa, sb, w_in, w_out, act, slope, *refs):
    blocks, (grad, total, gates, scaled) = refs[:-4], refs[-4:]
    s = jnp.concatenate([cut(blocks[:experts], *sa), cut(blocks[experts:], *sb)], axis=1)
    scaled[...] = s
    sums = 0.0
    for at, size in steps(w_out.shape[0], 256):
        up = dot(w_out[at : at + size, :], s, NT)
        sums = sums + gate_sums(act[at : at + size, :], up)
        grad[at : at + size, :] = (up * slope[at : at + size, :].astype(f32)).astype(bf16)
    gates[...] = sums
    for at, size in steps(w_in.shape[1], 256):
        total[:, at : at + size] = dot(grad[...], w_in[:, at : at + size], TN)


def far_kernel(block, capacity, pos, w_in, w_out, act, slope, near_total, near_gates, scaled, *refs):
    outs, (total, gates) = refs[:-2], refs[-2:]
    step, last = pl.program_id(0), pl.num_programs(0) - 1

    @pl.when(step == 0)
    def _():
        total[...] = near_total[...]
        gates[...] = near_gates[...]

    up = dot(w_out[...], scaled[...], NT)
    gates[...] += gate_sums(act[...], up)
    total[...] += dot((up * slope[...].astype(f32)).astype(bf16), w_in[...], TN)

    @pl.when(step == last)
    def _():
        rows = total[...].astype(bf16)
        gate_rows = gates[...].astype(bf16)
        for k, out in enumerate(outs):
            out[...] = rows[k * block : (k + 1) * block]
            out[capacity : capacity + 1, 0:block] = gate_rows[:, k * block : (k + 1) * block]


def cut(refs, left, size):
    return jnp.concatenate([ref[:, left : left + size] for ref in refs], axis=0)


def away_kernel(experts, owners, r, left, right, pos, own, other, *refs):
    out = refs[-1]
    size = own.shape[0] // owners
    mine = pl.ds(pl.multiple_of(lax.rem(pos[1] + r, owners) * size, size), size)
    for at, run in steps(out.shape[1], 256):
        total = dot(own[mine, :], cut(refs[:experts], left + at, run))
        total += dot(other[mine, :], cut(refs[experts : 2 * experts], right + at, run))
        out[:, at : at + run] = total.astype(out.dtype)


def home_kernel(experts, owners, parts, pos, own, other, *refs):
    out, total, sems = refs[-3:]
    size = own.shape[0] // owners
    mine = pl.ds(pl.multiple_of(pos[1] * size, size), size)
    per, column, copies = 2 * experts + owners - 1, 0, []
    for number, (left, right, extent) in enumerate(parts):
        blocks = refs[number * per : (number + 1) * per]
        for at, run in steps(extent, 256):
            rows = dot(own[mine, :], cut(blocks[:experts], left + at, run))
            rows += dot(other[mine, :], cut(blocks[experts : 2 * experts], right + at, run))
            for ref in blocks[2 * experts :]:
                rows += ref[:, at : at + run].astype(f32)
            total[:, column : column + run] = rows
            here = slice(column, column + run)
            copy = pltpu.make_async_copy(
                total.at[:, here], out.at[0, :, here], sems.at[len(copies)]
            )
            copy.start()
            copies.append(copy)
            column += run
    for copy in copies:
        copy.wait()


def after_kernel(owners, before, *refs):
    total = before[...]
    for ref in refs[: owners - 1]:
        total = total + ref[...].astype(f32)
    refs[-1][0] = total


def gathered(meta, refs, experts, block):
    first, second = picks(meta[0:1, :], meta[1:2, :], experts * block)
    chosen = jnp.where(first | second, 1.0, 0.0).astype(bf16)
    return dot(chosen, stack(refs, experts), TN)


def gate_rows(meta, refs, block, capacity):
    values = jnp.concatenate([ref[capacity : capacity + 1, 0:block] for ref in refs], axis=0)
    out = []
    for at in (0, 1):
        flat = meta[at : at + 1, :].astype(jnp.int32)
        live = flat >= 0
        which = jnp.where(live, flat, 0) // block
        where = flat - which * block
        lane = lax.broadcasted_iota(jnp.int32, (block, flat.shape[1]), 0)
        hit = jnp.where((lane == where) & live, 1.0, 0.0).astype(bf16)
        by_block = dot(values, hit)
        mine = lax.broadcasted_iota(jnp.int32, by_block.shape, 0) == which
        gate = jnp.sum(jnp.where(mine, by_block, 0.0), axis=0, keepdims=True)
        out.append(jnp.where(live, gate / meta[at + 2 : at + 3, :], 0.0))
    return out


def collect_kernel(experts, block, capacity, meta, *refs):
    blocks, (grad_tokens, grad_combine) = refs[:experts], refs[experts:]
    grad_tokens[...] = gathered(meta, blocks, experts, block).astype(bf16)

    @pl.when(pl.program_id(0) == 0)
    def _():
        gates = gate_rows(meta, blocks, block, capacity)
        grad_combine[...] = jnp.concatenate(gates, axis=0).astype(bf16)


def shaped(shape, dtype=bf16):
    return jax.ShapeDtypeStruct(shape, dtype)


def full(array):
    return pl.BlockSpec(array.shape, lambda g, *pos, rank=array.ndim: (0,) * rank)


def columns(array, parts, first=0):
    size = array.shape[-1] // parts
    lead = array.shape[:-1]
    return pl.BlockSpec(
        lead + (size,), lambda g, *pos, rank=array.ndim: (0,) * (rank - 1) + (first + g,)
    )


def rows(array, size):
    return pl.BlockSpec((size, array.shape[1]), lambda g, *pos: (g, 0))


def half_rows(array, parts, far=0):
    size = array.shape[1] // 2 // parts
    return pl.BlockSpec(
        (None, size, array.shape[2]), lambda g, pos: (0, (pos[0] ^ far) * parts + g, 0)
    )


def call(kernel, grid, scalars, operands, results, scratch=(), flops=0, alias=None):
    arrays, in_specs = [a for a, _ in operands], [s for _, s in operands]
    outs, out_specs = [a for a, _ in results], [s for _, s in results]
    moved = sum(a.size * a.dtype.itemsize for a in arrays + outs)
    return pl.pallas_call(
        kernel,
        out_shape=outs,
        grid_spec=pltpu.PrefetchScalarGridSpec(
            num_scalar_prefetch=len(scalars),
            grid=(grid,),
            in_specs=in_specs,
            out_specs=out_specs,
            scratch_shapes=list(scratch),
        ),
        input_output_aliases=alias or {},
        compiler_params=pltpu.CompilerParams(vmem_limit_bytes=28 << 20),
        cost_estimate=pl.CostEstimate(flops=int(flops), transcendentals=0, bytes_accessed=moved),
    )(*scalars, *arrays)


def direct(kernel, scalars, arrays, outs, flops=0):
    moved = sum(a.size * a.dtype.itemsize for a in list(arrays) + outs)
    return pl.pallas_call(
        kernel,
        out_shape=outs,
        in_specs=[pl.BlockSpec(memory_space=pltpu.SMEM)] * len(scalars)
        + [pl.BlockSpec(memory_space=pltpu.VMEM)] * len(arrays),
        out_specs=[pl.BlockSpec(memory_space=pltpu.VMEM)] * len(outs),
        compiler_params=pltpu.CompilerParams(vmem_limit_bytes=28 << 20),
        cost_estimate=pl.CostEstimate(flops=int(flops), transcendentals=0, bytes_accessed=moved),
    )(*scalars, *arrays)


def window(arrays, start, size):
    return [
        (a, pl.BlockSpec((a.shape[0], size), lambda g, *pos: (0, start // size))) for a in arrays
    ]


def runs_of(arrays, start, run):
    return [
        (a, pl.BlockSpec((a.shape[0], run), lambda g, *pos: (0, start // run + g))) for a in arrays
    ]


def per_device(tokens, grad_out, routes, keep_second, combine, w_in, w_out):
    experts, planes = lax.axis_size("expert"), lax.axis_size("dp")
    count, width = tokens.shape
    capacity = 5 * count // (2 * experts)
    block = -(-(capacity + 1) // 16) * 16
    owners = planes // 2
    units = w_in.shape[1] // 2
    share = units // owners
    slots = experts * block
    if planes % 2 or experts & (experts - 1):
        raise ValueError("mesh sizes")
    plane = lax.axis_index("dp")
    pos = jnp.stack([plane // owners, plane % owners]).astype(jnp.int32)
    bind = functools.partial

    def across(value):
        return lax.ppermute(value, "dp", [(j, (j + owners) % planes) for j in range(planes)])

    def exchange(values, which=None):
        sent = [
            lax.ppermute(values[k], "expert", [(i, i ^ k) for i in range(experts)])
            for k in which or range(1, experts)
        ]
        return sent if which else [values[0]] + sent

    def to_owners(values):
        return [
            lax.ppermute(
                value,
                "dp",
                [(j, j // owners * owners + (j + r + 1) % owners) for j in range(planes)],
            )
            for r, value in enumerate(values)
        ]

    def each(arrays, spec, *more):
        return [(a, spec(a, *more)) for a in arrays]

    routes_t, keep_t, combine_t = routes.T, keep_second.reshape(1, count), combine.T

    def stay(array):
        return pltpu.with_memory_space_constraint(array, pltpu.HBM)

    other_x = across(tokens)
    half = width // 2
    rest = width - half
    half = width // 2
    rest = width - half

    def blocks(columns_of):
        return [shaped((block, columns_of))] * experts

    act_shape = shaped((units, slots))
    unit_parts = max(units // 256, 1)
    unit_rows = units // unit_parts
    meta_shape = shaped((8, count), f32)
    meta, dya, dyb, *own_xs = call(
        bind(own_send_kernel, experts, block, capacity),
        1,
        [],
        each([stay(a) for a in (routes_t, keep_t, combine_t, tokens, grad_out)], full),
        each(
            [meta_shape, shaped((count, half)), shaped((count, rest))] + blocks(width + half),
            full,
        ),
        flops=3 * slots * count * width,
    )
    own_xs = exchange(own_xs)
    half_in, half_out = call(
        load_kernel,
        4,
        [pos],
        each([stay(w_in), stay(w_out)], half_rows, 4),
        each([shaped((units, width))] * 2, rows, units // 4),
    )
    other_dya = across(dya)
    other_dyb = across(dyb)
    other_meta = across(meta)
    other_xb = call(
        bind(send_x_kernel, experts, block),
        2,
        [],
        each([other_meta], full) + each([other_x], columns, 2),
        each(blocks(width), columns, 2),
        flops=2 * slots * count * width,
    )
    x_out = exchange(other_xb)
    sb_out = call(
        bind(send_s_kernel, experts, block, 0),
        1,
        [],
        each([meta, dyb], full),
        window(blocks(2 * rest), 0, rest),
        flops=slots * count * width,
    )
    sa_out = call(
        bind(send_s_kernel, experts, block, 0),
        1,
        [],
        each([other_meta, other_dya], full),
        each(blocks(half), full),
        flops=slots * count * width,
    )
    sa_out = exchange(sa_out)
    sb_out = call(
        bind(send_s_kernel, experts, block, 0),
        1,
        [],
        each([other_meta, other_dyb], full)
        + [(a, pl.BlockSpec(memory_space=pl.ANY)) for a in sb_out],
        window(blocks(2 * rest), rest, rest),
        flops=slots * count * width,
        alias={2 + k: k for k in range(experts)},
    )
    near = experts * 3 // 4
    sb_far = exchange(sb_out, range(near, experts))
    sb_out = [sb_out[0]] + exchange(sb_out, range(1, near)) + sb_far
    own_x, other_x = (own_xs, 0), (x_out, 0)
    own_sa, other_sa = (own_xs, width), (sa_out, 0)
    own_sb, other_sb = (sb_out, 0), (sb_out, rest)

    def act(x):
        return direct(
            bind(act_kernel, x[1]), [], [half_in] + x[0], [act_shape] * 2, 2 * slots * units * width
        )

    own_act, own_slope = act(own_x)
    other_act, other_slope = act(other_x)
    far_act, far_slope = call(
        bind(far_act_kernel, experts),
        unit_parts,
        [pos],
        each([stay(w_in)], half_rows, unit_parts, 1) + window(*own_x, width),
        each([act_shape] * 2, rows, unit_rows),
        flops=2 * slots * units * width,
    )
    run = width // 4
    fed = slots * share * run

    def away(acts, left, right, first, extent):
        return [
            direct(
                bind(away_kernel, experts, owners, r, left[1] + first, right[1] + first),
                [pos],
                acts + left[0] + right[0],
                [shaped((share, extent))],
                4 * slots * share * extent,
            )[0]
            for r in range(1, owners)
        ]

    goal = shaped((1, share, width), f32)

    def into(array, operands, prefetched):
        if array is None:
            return operands, None
        return operands + [(array, pl.BlockSpec(memory_space=pl.ANY))], {
            len(operands) + prefetched: 0
        }

    def after(before, got, first, many, array=None):
        operands, alias = into(
            array, runs_of([before], first * run, run) + each(got, columns, many), 0
        )
        return call(
            bind(after_kernel, owners),
            many,
            [],
            operands,
            each([goal], columns, 4, first),
            alias=alias,
        )[0]

    out_acts = [own_act, other_act]
    away_oa = away(out_acts, own_sa, other_sa, 0, half)
    got_oa = to_owners(away_oa)
    early = rest // 4
    away_ob = away(out_acts, own_sb, other_sb, 0, early)
    got_ob = to_owners(away_ob)
    away_oc = away(out_acts, own_sb, other_sb, early, rest - early)
    got_oc = to_owners(away_oc)
    total_shape, gate_shape = shaped((slots, width), f32), shaped((1, slots), f32)
    own_grad, near_total, near_gates, own_scaled = direct(
        bind(own_grad_kernel, experts, (own_sa[1], half), (own_sb[1], rest)),
        [],
        [half_in, half_out, own_act, own_slope] + own_sa[0] + own_sb[0],
        [act_shape, total_shape, gate_shape, shaped((slots, width))],
        4 * slots * units * width,
    )
    other_grad = direct(
        bind(other_grad_kernel, experts, (other_sa[1], half), (other_sb[1], rest)),
        [],
        [half_out, other_slope] + other_sa[0] + other_sb[0],
        [act_shape],
        2 * slots * units * width,
    )[0]
    own_back = call(
        bind(far_kernel, block, capacity),
        unit_parts,
        [pos],
        each([stay(w_in), stay(w_out)], half_rows, unit_parts, 1)
        + each([far_act, far_slope], rows, unit_rows)
        + each([near_total, near_gates, own_scaled], full),
        each(blocks(width), full),
        [pltpu.VMEM((slots, width), f32), pltpu.VMEM((1, slots), f32)],
        4 * slots * units * width,
    )
    in_acts = [own_grad, other_grad]
    away_a = away(in_acts, own_x, other_x, 0, 3 * run)
    got_a = to_owners(away_a)
    away_b = away(in_acts, own_x, other_x, 3 * run, run)
    got_b = to_owners(away_b)
    own_back = exchange(own_back)

    operands = (
        out_acts
        + own_sa[0]
        + other_sa[0]
        + got_oa
        + own_sb[0]
        + other_sb[0]
        + got_ob
        + own_sb[0]
        + other_sb[0]
        + got_oc
    )
    parts = (
        (own_sa[1], other_sa[1], half),
        (own_sb[1], other_sb[1], early),
        (own_sb[1] + early, other_sb[1] + early, rest - early),
    )
    grad_outw = pl.pallas_call(
        bind(home_kernel, experts, owners, parts),
        name="home_out",
        out_shape=goal,
        in_specs=[pl.BlockSpec(memory_space=pltpu.SMEM)]
        + [pl.BlockSpec(memory_space=pltpu.VMEM)] * len(operands),
        out_specs=pl.BlockSpec(memory_space=pl.ANY),
        scratch_shapes=[
            pltpu.VMEM((share, width), f32),
            pltpu.SemaphoreType.DMA((sum(len(steps(part[2], 256)) for part in parts),)),
        ],
        compiler_params=pltpu.CompilerParams(vmem_limit_bytes=28 << 20),
        cost_estimate=pl.CostEstimate(
            flops=4 * slots * share * width, transcendentals=0, bytes_accessed=12 * share * width
        ),
    )(pos, *operands)
    grad_tokens, grad_combine = call(
        bind(collect_kernel, experts, block, capacity),
        2,
        [],
        each([meta], full) + each(own_back, columns, 2),
        each([shaped((count, width))], columns, 2) + each([shaped((2, count))], full),
        flops=2 * slots * count * width,
    )
    before = direct(
        bind(away_kernel, experts, owners, 0, own_x[1], other_x[1]),
        [pos],
        in_acts + own_x[0] + other_x[0],
        [shaped((share, width), f32)],
        16 * fed,
    )[0]
    grad_in = after(before, got_a, 0, 3)
    grad_in = after(before, got_b, 3, 1, grad_in)
    return grad_tokens, grad_combine.T, grad_in, grad_outw


def solution(mesh):
    return jax.shard_map(
        per_device,
        mesh=mesh,
        in_specs=(
            P(("expert", "dp"), None),
            P(("expert", "dp"), None),
            P(("expert", "dp"), None),
            P(("expert", "dp")),
            P(("expert", "dp"), None),
            P("expert", None, None),
            P("expert", None, None),
        ),
        out_specs=(
            P(("expert", "dp"), None),
            P(("expert", "dp"), None),
            P("expert", "dp", None),
            P("expert", "dp", None),
        ),
        check_vma=False,
    )
```
